256 devices in a mesh: tile: 64 (over x, y, z_hi), view: 4 (over z_lo, core).
Axes of the slice: x: 4, y: 4, z: 8 (z_hi: 4, z_lo: 2; z = z_hi * 2 + z_lo), core: 2. Of those that a mesh axis runs over, the one named last changes fastest.
Arguments:
- initial: float32 [64, 4, 256, 256], P('tile'), may hold values from 0.5 to 2
- recorded: float32 [4, 64, 4, 256, 256], P('view', 'tile'), may hold values from 0.2 to 3
- tap_table: float32 [4, 8, 3, 31], P('view'), may hold values from 0.02 to 1
- variants: int32 [4, 64], P('view'), may hold values from 0 to 7
Outputs:
- estimate: float32 [64, 4, 256, 256], P('tile')
The draws below stay inside these ranges and needn't reach their ends.
Inputs may be any that keep to these rules, and one draw needn't show every extreme that they name: `variants`: indices of the 8 tap tables of the view.
All inputs are finite; a program needn't handle non-finite values.
Results may differ from the reference program's by a relative error of at most 0.0001.
Values sent between devices are 32-bit elements; how exact they have to be, the bound alone decides.
No kernel may reach another device: no remote copies, remote signals or barrier semaphores. Data moves between devices by JAX's collectives and lax.ppermute only.
A program may use at most 192 MiB of HBM per device.

```python
import math
import jax
import jax.numpy as jnp
from jax import lax

Z = 4
TY = 256
TX = 256
GX = 8
TAPS = 31
VARIANTS = 8
ITERS = 2
HALF = 15
VIEWS = 4
N_TILE = 64
N_VIEW = 4


def place_ends(values, own_key, smallest, largest):
    longest = values.shape.index(max(values.shape))
    spots = []
    for shift in (0, 1):
        where = [jax.random.randint(jax.random.fold_in(own_key, axis), (), 0, length) for axis, length in enumerate(values.shape)]
        where[longest] = (where[longest] + shift) % values.shape[longest]
        spots.append(tuple(where))
    return values.at[spots[0]].set(smallest).at[spots[1]].set(largest)


def levels(stream_key, dims, cuts, low, high):
    level = 1.0
    for position, shards_of in cuts:
        draws = jax.random.uniform(jax.random.fold_in(jax.random.fold_in(stream_key, 6), position), (shards_of,), jnp.float32, low / len(cuts), high / len(cuts))
        level = level * jnp.repeat(jnp.exp(draws), dims[position] // shards_of).reshape((-1,) + (1,) * (len(dims) - 1 - position))
    return level


def setup_inputs(seed: int = 0) -> dict:
    key_of = jax.random.split(jax.random.key(seed), 5)
    return {
        "initial": jnp.clip(0.5 + 1.5 * jax.random.uniform(key_of[0], (N_TILE, Z, TY, TX), jnp.float32) ** levels(key_of[0], (N_TILE, Z, TY, TX), ((0, 64),), -0.2, 0.2), 0.5, 2.0),
        "recorded": jnp.clip(0.2 + 2.8 * jax.random.uniform(key_of[1], (VIEWS, N_TILE, Z, TY, TX), jnp.float32) ** levels(key_of[1], (VIEWS, N_TILE, Z, TY, TX), ((0, 4), (1, 64)), -0.2, 0.2), 0.2, 3.0),
        "tap_table": jnp.clip(jnp.exp(math.log(1.0) - 3.912023 * jax.random.uniform(key_of[2], (VIEWS, VARIANTS, 3, TAPS), jnp.float32) ** levels(key_of[2], (VIEWS, VARIANTS, 3, TAPS), ((0, 4),), -0.2, 0.2)), 0.02, 1.0),
        "variants": place_ends(jax.random.randint(key_of[3], (VIEWS, N_TILE), 0, VARIANTS), jax.random.fold_in(key_of[3], 1), 0, VARIANTS - 1).astype(jnp.int32),
    }


def normalized(tap_table):
    return tap_table / jnp.sum(tap_table, axis=-1, keepdims=True)


def tile_kernels(kernels, variant_ids, grid_rows, grid_cols):
    count_variants = kernels.shape[0]
    onehot = (variant_ids[:, None] == jnp.arange(count_variants, dtype=jnp.int32)[None, :]).astype(jnp.float32)
    flat = jnp.dot(onehot, kernels.reshape(count_variants, -1), precision=lax.Precision.HIGHEST)
    return flat.reshape(grid_rows, grid_cols, 3, kernels.shape[-1])


def tile_onehot(positions, extent, count):
    owner = jnp.clip(jnp.floor_divide(positions, extent), 0, count - 1).astype(jnp.int32)
    return (owner[:, None] == jnp.arange(count, dtype=jnp.int32)[None, :]).astype(jnp.float32)


def weight_map(tile_taps, axis_id, offset, row_hot, col_hot):
    inner = jnp.dot(row_hot, tile_taps[:, :, axis_id, offset], precision=lax.Precision.HIGHEST)
    return jnp.dot(inner, col_hot.T, precision=lax.Precision.HIGHEST)


def blur_cols(padded, tile_taps, row_hot, col_hot):
    count = col_hot.shape[0]
    result = jnp.zeros((padded.shape[0], padded.shape[1], count), jnp.float32)
    for offset in range(tile_taps.shape[3]):
        weights = weight_map(tile_taps, 0, offset, row_hot, col_hot)
        result = result + weights[None] * padded[:, :, offset:offset + count]
    return result


def blur_rows(padded, tile_taps, row_hot, col_hot):
    count = row_hot.shape[0]
    result = jnp.zeros((padded.shape[0], count, padded.shape[2]), jnp.float32)
    for offset in range(tile_taps.shape[3]):
        weights = weight_map(tile_taps, 1, offset, row_hot, col_hot)
        result = result + weights[None] * padded[:, offset:offset + count, :]
    return result


def blur_planes(field, tile_taps, row_hot, col_hot, reverse):
    taps = tile_taps.shape[3]
    margin = taps // 2
    padded = jnp.pad(field, ((margin, margin), (0, 0), (0, 0)))
    planes = field.shape[0]
    result = jnp.zeros(field.shape, jnp.float32)
    for offset in range(taps):
        which = taps - 1 - offset if reverse else offset
        weights = weight_map(tile_taps, 2, which, row_hot, col_hot)
        result = result + weights[None] * padded[offset:offset + planes]
    return result


def adjoint_rows(padded, tile_taps, row_hot, col_hot):
    margin = tile_taps.shape[3] // 2
    count = padded.shape[1] - 2 * margin
    result = jnp.zeros((padded.shape[0], count, padded.shape[2]), jnp.float32)
    for offset in range(tile_taps.shape[3]):
        lead = 2 * margin - offset
        weights = weight_map(tile_taps, 1, offset, row_hot, col_hot)
        result = result + weights[None, lead:lead + count, :] * padded[:, lead:lead + count, :]
    return result


def adjoint_cols(padded, tile_taps, row_hot, col_hot):
    margin = tile_taps.shape[3] // 2
    count = padded.shape[2] - 2 * margin
    result = jnp.zeros((padded.shape[0], padded.shape[1], count), jnp.float32)
    for offset in range(tile_taps.shape[3]):
        lead = 2 * margin - offset
        weights = weight_map(tile_taps, 0, offset, row_hot, col_hot)
        result = result + weights[None, :, lead:lead + count] * padded[:, :, lead:lead + count]
    return result


def assemble(blocks, grid_rows):
    shaped = blocks.reshape(grid_rows, GX, Z, TY, TX)
    return shaped.transpose(2, 0, 3, 1, 4).reshape(Z, grid_rows * TY, GX * TX)


def disassemble(field, grid_rows):
    shaped = field.reshape(Z, grid_rows, TY, GX, TX)
    return shaped.transpose(1, 3, 0, 2, 4).reshape(grid_rows * GX, Z, TY, TX)


def reference(initial, recorded, tap_table, variants):
    grid_rows = N_TILE // GX
    estimate = assemble(initial, grid_rows)
    count_rows = grid_rows * TY
    count_cols = GX * TX
    own_rows = tile_onehot(jnp.arange(count_rows, dtype=jnp.int32), TY, grid_rows)
    own_cols = tile_onehot(jnp.arange(count_cols, dtype=jnp.int32), TX, GX)
    wide_rows = tile_onehot(jnp.arange(count_rows + 2 * HALF, dtype=jnp.int32) - HALF, TY, grid_rows)
    wide_cols = tile_onehot(jnp.arange(count_cols + 2 * HALF, dtype=jnp.int32) - HALF, TX, GX)
    for step in range(ITERS):
        logged = jnp.zeros(estimate.shape, jnp.float32)
        for view in range(N_VIEW):
            tile_taps = tile_kernels(normalized(tap_table[view]), variants[view], grid_rows, GX)
            observed = assemble(recorded[view], grid_rows)
            padded = jnp.pad(estimate, ((0, 0), (0, 0), (HALF, HALF)))
            planes = blur_planes(blur_cols(padded, tile_taps, own_rows, own_cols), tile_taps, own_rows, own_cols, False)
            blurred = blur_rows(jnp.pad(planes, ((0, 0), (HALF, HALF), (0, 0))), tile_taps, own_rows, own_cols)
            ratio = observed / blurred
            back = adjoint_rows(jnp.pad(ratio, ((0, 0), (HALF, HALF), (0, 0))), tile_taps, wide_rows, own_cols)
            back = blur_planes(back, tile_taps, own_rows, own_cols, True)
            correction = adjoint_cols(jnp.pad(back, ((0, 0), (0, 0), (HALF, HALF))), tile_taps, own_rows, wide_cols)
            logged = logged + jnp.log(correction)
        estimate = estimate * jnp.exp(logged / N_VIEW)
    return disassemble(estimate, grid_rows)
```

```python
import functools

import jax
import jax.numpy as jnp
from jax import lax
from jax.experimental import pallas as pl
from jax.experimental.pallas import tpu as pltpu
from jax.sharding import PartitionSpec as P

GX = 8
ITERS = 2
HALF = 15
F32 = jnp.float32
BF16 = jnp.bfloat16
VMEM = pltpu.VMEM
SMEM = pltpu.SMEM


def call(body, outs, scratch, *args, cost=None):
    specs = [pl.BlockSpec(memory_space=SMEM)] + [pl.BlockSpec(memory_space=VMEM)] * (len(args) - 1)
    return pl.pallas_call(
        body,
        out_shape=outs,
        in_specs=specs,
        out_specs=jax.tree.map(lambda _: pl.BlockSpec(memory_space=VMEM), outs),
        scratch_shapes=scratch,
        compiler_params=pltpu.CompilerParams(vmem_limit_bytes=52 * 1024 * 1024),
        cost_estimate=cost,
    )(*args)


def shape(*dims, dtype=F32):
    return jax.ShapeDtypeStruct(dims, dtype)


def lanes(rows, width=128):
    return lax.broadcasted_iota(jnp.int32, (rows, width), 1)


def turn(x, amount):
    amount = amount % x.shape[-1]
    return x if amount == 0 else pltpu.roll(x, amount, axis=x.ndim - 1)


def packed(pieces, first, width):
    rows = pieces[0].shape[0]
    lane = lanes(rows)
    out = jnp.zeros((rows, 128), F32)
    for n, piece in enumerate(pieces):
        inside = (lane >= n * width) & (lane < (n + 1) * width)
        out = jnp.where(inside, turn(piece, n * width - first), out)
    return out


def split(x):
    high = x.astype(BF16)
    return high, (x - high.astype(F32)).astype(BF16)


def dot3(a, b):
    (ah, al), (bh, bl) = a, b
    dot = functools.partial(jnp.dot, preferred_element_type=F32)
    return dot(ah, bh) + (dot(al, bh) + dot(ah, bl))


def pack_kernel(info, rec, first, taps, sent, main, inside, edge):
    view = info[0]
    for q in range(4):
        qx, qy = q // 2, q % 2
        rows = slice(112 * qy, 112 * qy + 144)
        slot = jnp.bitwise_xor(view, q)
        for z in range(4):
            sent[slot, z] = rec[z, rows, 128 * qx : 128 * qx + 128]
        near = [rec[z, rows, 128 - 128 * qx : 256 - 128 * qx] for z in range(4)]
        side = packed(near, 112 * qx, 16)
        sent[slot, 4, 16:] = side[16:]
        sent[slot, 4, :16] = side[:16] + taps[q]

        @pl.when(view == q)
        def _():
            span = slice(96 * qy, 96 * qy + 160)
            for z in range(4):
                main[z] = first[z, span, 128 * qx : 128 * qx + 128]
            beside = [first[z, span, 128 - 128 * qx : 256 - 128 * qx] for z in range(4)]
            inside[...] = packed(beside, 96 * qx, 32)
            own = [first[z, span, 128 * qx : 128 * qx + 128] for z in range(4)]
            edge[...] = packed(own, 96 * qx, 32)


def pack_cols_kernel(info, got, edge, out):
    qx = info[1]
    for side in range(2):

        @pl.when(qx == side)
        def _():
            for h in range(2):
                pieces = [got[(2 * h + s) ^ 2, z] for s in range(2) for z in range(4)]
                out[h * 144 : h * 144 + 144] = packed(pieces, 112 * side, 16)

    out[288:] = edge[...]


def pack_rows_kernel(info, got, cols, main, inside, out):
    qy = info[2]
    low = lanes(16) < 64
    for side in range(2):

        @pl.when(qy == side)
        def _():
            rows = slice(128 * side, 128 * side + 16)
            for s in range(4):
                for z in range(4):
                    n = 4 * s + z
                    out[n * 16 : n * 16 + 16] = got[s ^ 1, z, rows]
            for h in range(2):
                one, two = got[2 * h + 1, 4, rows], got[2 * h, 4, rows]
                out[256 + 16 * h : 272 + 16 * h] = jnp.where(low, one, turn(two, 64))
                wide = cols[h * 144 + rows.start : h * 144 + rows.stop]
                out[288 + 16 * h : 304 + 16 * h] = turn(wide, 64)
            rows = slice(128 * side, 128 * side + 32)
            for z in range(4):
                out[320 + 32 * z : 352 + 32 * z] = main[z, rows]
            out[448:480] = inside[rows]
            out[480:512] = cols[288 + rows.start : 288 + rows.stop]


def toeplitz(base, shift):
    return pltpu.roll(base, shift % 256, axis=1, stride=1, stride_axis=0)


def matrices_kernel(info, got, xh, xl, ah, al, yh, yl, th, tl, zw):
    qx, qy = info[1], info[2]

    def far_lane(rows):
        lane = lanes(rows, 256)
        return (lane >= 128) & ((lane < 192) == (qx == 1))

    def body(s, carry):
        table = got[s, 4, 0:16]
        lane = lanes(16)
        fwd = jnp.where(lane < 31, turn(table, 64), 0.0)
        rev = jnp.where(lane < 31, turn(table, 32), 0.0)
        zero = jnp.zeros((16, 128), F32)
        fwd = jnp.concatenate([fwd, zero], 1)
        rev = jnp.concatenate([rev, zero], 1)

        def wide(which, tile, axis, rows):
            return jnp.broadcast_to(which[3 * tile + axis : 3 * tile + axis + 1], (rows, 256))

        def keep(high, low, index, value):
            high[index], low[index] = split(value)

        far = far_lane(256)
        for g in range(2):
            near_t = toeplitz(wide(rev, 2 * g, 0, 256), -HALF)
            far_t = toeplitz(wide(rev, 2 * g + 1, 0, 256), -HALF)
            keep(xh, xl, (s, g), jnp.where(far, far_t, near_t))
        row = lax.broadcasted_iota(jnp.int32, (256, 256), 0)
        far_row = (row >= 128) & ((row < 192) == (qx == 1))
        base = jnp.where(far_row, wide(fwd, 1, 0, 256), wide(fwd, 0, 0, 256))
        keep(ah, al, s, toeplitz(base, -HALF)[:, :128])
        for g in range(2):
            row = lax.broadcasted_iota(jnp.int32, (160, 256), 0)
            other = jnp.where(qy == 0, row, 159 - row) < 16
            base = jnp.where(other, wide(fwd, 2 + g, 1, 160), wide(fwd, g, 1, 160))
            keep(yh, yl, (s, g), toeplitz(base, 1))
            lane = lanes(128, 256)
            other = jnp.where(qy == 0, lane, 159 - lane) < 16
            near_t = toeplitz(wide(rev, g, 1, 128), 1)
            far_t = toeplitz(wide(rev, 2 + g, 1, 128), 1)
            keep(th, tl, (s, g), jnp.where(other, far_t, near_t))
        far = far_lane(1)
        for g in range(2):
            for d in range(7):
                near_w = fwd[6 * g + 2 : 6 * g + 3, 12 + d : 13 + d]
                far_w = fwd[6 * g + 5 : 6 * g + 6, 12 + d : 13 + d]
                weight = jnp.where(
                    far, jnp.broadcast_to(far_w, (1, 256)), jnp.broadcast_to(near_w, (1, 256))
                )
                zw[s, g, d : d + 1] = weight
        return carry

    lax.fori_loop(0, 4, body, 0)


def sided(left, right, width, n, rows):
    lane = lanes(rows)
    out = jnp.where(lane < width, turn(right, -n * width), 0.0)
    return jnp.where(lane >= 128 - width, turn(left, 128 - width - n * width), out)


def step_kernel(first, info, *refs):
    if first:
        (main, inside, cols, rows_in, got), refs = refs[:5], refs[5:]
    else:
        (main, inside, beyond, rows_in, rows_out, rec), refs = refs[:6], refs[6:]
    (xh, xl, ah, al, yh, yl, th, tl, zw), refs = refs[:9], refs[9:]
    if first:
        (out, near_edge, far_edge, rec), refs = refs[:4], refs[4:]
    else:
        (out,), refs = refs[:1], refs[1:]
    region, eh, el, mid, ph, plo, rh, rl, total = refs
    qx, qy = info[1], info[2]
    own = pl.multiple_of(32 * (1 - qy), 32)
    other = pl.multiple_of(160 * qy, 32)

    if first:
        for z in range(4):
            region[z, pl.ds(own, 160)] = main[z]
            region[z, pl.ds(other, 32)] = rows_in[320 + 32 * z : 352 + 32 * z]
        region[4, pl.ds(own, 160)] = inside[...]
        region[5, pl.ds(own, 160)] = cols[288:448]
        region[4, pl.ds(other, 32)] = rows_in[448:480]
        region[5, pl.ds(other, 32)] = rows_in[480:512]
    else:
        for z in range(4):
            region[z, 32:160] = main[z]
        region[4, 32:160] = inside[...]
        region[5, 32:160] = beyond[...]
        for p in range(6):
            region[p, pl.ds(pl.multiple_of(160 * (1 - qy), 32), 32)] = rows_in[p]
            region[p, pl.ds(other, 32)] = rows_out[p]
    left = jnp.where(qx == 0, region[5], region[4])
    right = jnp.where(qx == 0, region[4], region[5])
    for z in range(4):
        eh[z, :, :128], el[z, :, :128] = split(region[z])
        eh[z, :, 128:], el[z, :, 128:] = split(sided(left, right, 32, z, 192))

    if first:
        in_tile = pl.multiple_of(16 * (1 - qy), 16)
        out_tile = pl.multiple_of(144 * qy, 16)
        for s in range(4):
            h, m = s // 2, 4 * (s % 2)
            for z in range(4):
                rec[s, z, pl.ds(in_tile, 144), :128] = got[s, z]
                n = 4 * s + z
                rec[s, z, pl.ds(out_tile, 16), :128] = rows_in[n * 16 : n * 16 + 16]
            for at, count, inner, outer, shift in (
                (in_tile, 144, got[s, 4], cols[h * 144 : h * 144 + 144], 0),
                (
                    out_tile,
                    16,
                    rows_in[256 + 16 * h : 272 + 16 * h],
                    rows_in[288 + 16 * h : 304 + 16 * h],
                    64 * (s % 2),
                ),
            ):
                inner = turn(inner, -shift)
                outer = turn(outer, -16 * m)
                lhs = jnp.where(qx == 0, outer, inner)
                rhs = jnp.where(qx == 0, inner, outer)
                for z in range(4):
                    rec[s, z, pl.ds(at, count), 128:] = sided(lhs, rhs, 16, z, count)

    ph[:, 192:] = jnp.zeros((4, 64, 256), BF16)
    plo[:, 192:] = jnp.zeros((4, 64, 256), BF16)
    rh[:, 160:] = jnp.zeros((4, 96, 256), BF16)
    rl[:, 160:] = jnp.zeros((4, 96, 256), BF16)
    total[...] = jnp.zeros_like(total)

    lane = lanes(160, 256)
    row = lax.broadcasted_iota(jnp.int32, (160, 256), 0)
    used = (lane < 144) | (lane >= 240)
    far = (lane >= 128) & ((lane < 192) == (qx == 1))
    past = jnp.where(qy == 0, row, 159 - row) < 16
    valid = used & ((info[3] > 0) | ~far) & ((info[4] > 0) | ~past)
    far160 = far[:, 128:]
    far128 = far[:128, 128:]

    def body(s, carry):
        for g, at, count in ((0, own, 160), (1, other, 32)):
            for z in range(4):
                here = (eh[z, pl.ds(at, count)], el[z, pl.ds(at, count)])
                mid[z, pl.ds(at, count)] = dot3(here, (xh[s, g], xl[s, g]))
            weights = [zw[s, g, d : d + 1] for d in range(7)]
            planes = [mid[z, pl.ds(at, count)] for z in range(4)]
            for z in range(4):
                value = sum(weights[3 + k - z] * planes[k] for k in range(4))
                ph[z, pl.ds(at, count)], plo[z, pl.ds(at, count)] = split(value)
        y_own, y_far = (yh[s, 0], yl[s, 0]), (yh[s, 1], yl[s, 1])
        for z in range(4):
            blurred = dot3(y_own, (ph[z], plo[z]))
            edge = dot3(y_far, (ph[z, :, 128:], plo[z, :, 128:]))
            blurred = jnp.concatenate(
                [blurred[:, :128], jnp.where(far160, edge, blurred[:, 128:])], 1
            )
            ratio = jnp.where(valid, rec[s, z] / blurred, 0.0)
            rh[z, :160], rl[z, :160] = split(ratio)
        t_own, t_far = (th[s, 0], tl[s, 0]), (th[s, 1], tl[s, 1])
        planes = []
        for z in range(4):
            back = dot3(t_own, (rh[z], rl[z]))
            edge = dot3(t_far, (rh[z, :, 128:], rl[z, :, 128:]))
            mid[z, :128] = jnp.concatenate(
                [back[:, :128], jnp.where(far128, edge, back[:, 128:])], 1
            )
        weights = [zw[s, 0, d : d + 1] for d in range(7)]
        planes = [mid[z, :128] for z in range(4)]
        for z in range(4):
            value = sum(weights[3 + z - k] * planes[k] for k in range(4))
            correction = dot3(split(value), (ah[s], al[s]))
            total[z] += jnp.log(correction)
        return carry

    lax.fori_loop(0, 4, body, 0)
    new = []
    for z in range(4):
        value = region[z, 32:160] * jnp.exp(total[z] / 4)
        out[z] = value
        new.append(value)
    if first:
        low, high = packed(new, 0, 32), packed(new, 96, 32)
        near_edge[...] = jnp.where(qx == 0, high, low)
        far_edge[...] = jnp.where(qx == 0, low, high)


def per_device(initial, recorded, tap_table, variants):
    tile = lax.axis_index("tile")
    view = lax.axis_index("view")
    count_tiles = lax.axis_size("tile")
    grid_rows = count_tiles // GX
    tile_row, tile_col = tile // GX, tile % GX
    qx, qy = view // 2, view % 2
    has_x = jnp.where(qx == 0, tile_col > 0, tile_col < GX - 1)
    has_y = jnp.where(qy == 0, tile_row > 0, tile_row < grid_rows - 1)
    info = jnp.stack([view, qx, qy, has_x.astype(jnp.int32), has_y.astype(jnp.int32)])

    def route(x, pairs):
        return lax.ppermute(x, ("tile", "view"), pairs)

    def over_view(x, flip):
        return lax.ppermute(x, "view", [(i, i ^ flip) for i in range(4)])

    x_pairs, y_pairs = [], []
    for t in range(count_tiles):
        for v in range(4):
            if v // 2 and t % GX < GX - 1:
                x_pairs += [(4 * t + v, 4 * (t + 1) + v - 2), (4 * (t + 1) + v - 2, 4 * t + v)]
            if v % 2 and t + GX < count_tiles:
                y_pairs += [(4 * t + v, 4 * (t + GX) + v - 1), (4 * (t + GX) + v - 1, 4 * t + v)]

    kernels = tap_table[0] / jnp.sum(tap_table[0], axis=-1, keepdims=True)
    steps_x = jnp.array([[0, d, 0, d] for d in (-1, -1, 1, 1)], jnp.int32)
    steps_y = jnp.array([[0, 0, d, d] for d in (-1, 1, -1, 1)], jnp.int32)
    near_x = jnp.clip(tile_col + steps_x, 0, GX - 1)
    near_y = jnp.clip(tile_row + steps_y, 0, grid_rows - 1)
    near = (near_y * GX + near_x).reshape(16)
    ids = jnp.sum(
        jnp.where(near[:, None] == jnp.arange(count_tiles)[None], variants[0][None], 0), axis=1
    )
    picked = ids[:, None] == jnp.arange(kernels.shape[0])[None]
    taps = jnp.sum(jnp.where(picked[:, :, None, None], kernels[None], 0.0), axis=1)
    taps = taps.reshape(4, 12, 31)
    taps = jnp.concatenate([jnp.pad(taps, ((0, 0), (0, 0), (64, 1))), taps[..., ::-1]], axis=-1)
    taps = jnp.pad(taps, ((0, 0), (0, 4), (0, 1)))

    sent, main, inside, edge = call(
        pack_kernel,
        (shape(4, 5, 144, 128), shape(4, 160, 128), shape(160, 128), shape(160, 128)),
        [],
        info,
        recorded[0, 0],
        initial[0],
        taps,
    )
    got = jnp.stack([sent[0]] + [over_view(sent[s], s) for s in (1, 2, 3)])
    cols = route(call(pack_cols_kernel, shape(448, 128), [], info, got, edge), x_pairs)
    mats = call(
        matrices_kernel,
        tuple(
            shape(4, *dims, dtype=BF16)
            for dims in ((2, 256, 256), (256, 128), (2, 160, 256), (2, 128, 256))
            for _ in range(2)
        )
        + (shape(4, 2, 8, 256),),
        [],
        info,
        got,
    )
    rows = route(
        call(pack_rows_kernel, shape(512, 128), [], info, got, cols, main, inside), y_pairs
    )
    scratch = [
        VMEM((6, 192, 128), F32),
        VMEM((4, 192, 256), BF16),
        VMEM((4, 192, 256), BF16),
        VMEM((4, 192, 256), F32),
        VMEM((4, 256, 256), BF16),
        VMEM((4, 256, 256), BF16),
        VMEM((4, 256, 256), BF16),
        VMEM((4, 256, 256), BF16),
        VMEM((4, 128, 128), F32),
    ]
    quad = shape(4, 128, 128)
    cost = pl.CostEstimate(flops=8_000_000_000, bytes_accessed=12_000_000, transcendentals=600_000)
    estimate, near_edge, far_edge, rec = call(
        functools.partial(step_kernel, True),
        (quad, shape(128, 128), shape(128, 128), shape(4, 4, 160, 256)),
        scratch,
        info,
        main,
        inside,
        cols,
        rows,
        got,
        *mats,
        cost=cost,
    )
    for step in range(1, ITERS):
        inside = over_view(near_edge, 2)
        beyond = route(far_edge, x_pairs)
        whole = jnp.concatenate([estimate, inside[None], beyond[None]])
        low, high = whole[:, :32], whole[:, 96:]
        rows_in = over_view(jnp.where(qy == 0, high, low), 1)
        rows_out = route(jnp.where(qy == 0, low, high), y_pairs)
        estimate = call(
            functools.partial(step_kernel, False),
            quad,
            scratch,
            info,
            estimate,
            inside,
            beyond,
            rows_in,
            rows_out,
            rec,
            *mats,
            cost=cost,
        )
    across = over_view(estimate, 2)
    wide = jnp.where(
        qx == 0,
        jnp.concatenate([estimate, across], 2),
        jnp.concatenate([across, estimate], 2),
    )
    down = over_view(wide, 1)
    return jnp.where(
        qy == 0, jnp.concatenate([wide, down], 1), jnp.concatenate([down, wide], 1)
    )[None]


def solution(mesh):
    return jax.shard_map(
        per_device,
        mesh=mesh,
        in_specs=(
            P("tile", None, None, None),
            P("view", "tile", None, None, None),
            P("view", None, None, None),
            P("view", None),
        ),
        out_specs=P("tile", None, None, None),
        check_vma=False,
    )
```

```python
import functools

import jax
import jax.numpy as jnp
from jax import lax
from jax.experimental import pallas as pl
from jax.experimental.pallas import tpu as pltpu
from jax.sharding import PartitionSpec as P

GX = 8
ITERS = 2
HALF = 15
F32 = jnp.float32
BF16 = jnp.bfloat16
VMEM = pltpu.VMEM
SMEM = pltpu.SMEM


def call(body, outs, scratch, scalars, *args, flops=0):
    specs = [pl.BlockSpec(memory_space=SMEM)] * len(scalars)
    specs += [pl.BlockSpec(memory_space=VMEM)] * len(args)
    moved = sum(a.size * a.dtype.itemsize for a in args)
    return pl.pallas_call(
        body,
        out_shape=outs,
        in_specs=specs,
        out_specs=jax.tree.map(lambda _: pl.BlockSpec(memory_space=VMEM), outs),
        scratch_shapes=scratch,
        compiler_params=pltpu.CompilerParams(vmem_limit_bytes=48 * 1024 * 1024),
        cost_estimate=pl.CostEstimate(flops=flops, bytes_accessed=moved, transcendentals=0),
    )(*scalars, *args)


def shape(*dims, dtype=F32):
    return jax.ShapeDtypeStruct(dims, dtype)


def lanes(rows, width=128):
    return lax.broadcasted_iota(jnp.int32, (rows, width), 1)


def turn(x, amount):
    if isinstance(amount, int):
        amount = amount % x.shape[-1]
        if amount == 0:
            return x
    return pltpu.roll(x, amount, axis=x.ndim - 1)


def packed(pieces, first, width):
    rows = pieces[0].shape[0]
    lane = lanes(rows)
    out = jnp.zeros((rows, 128), F32)
    for n, piece in enumerate(pieces):
        inside = (lane >= n * width) & (lane < (n + 1) * width)
        out = jnp.where(inside, turn(piece, n * width - first), out)
    return out


def right_half(rows):
    return lax.rem(lanes(rows), 32) < 16


def shared(pieces, qx):
    rows = pieces[0].shape[0]
    lane = lanes(rows)
    out = jnp.zeros((rows, 128), F32)
    for z, piece in enumerate(pieces):
        mine = jnp.where(qx == 0, turn(piece, 32 * z), turn(piece, 32 * z + 32))
        out = jnp.where((lane >= 32 * z) & (lane < 32 * z + 32), mine, out)
    return jnp.where(right_half(rows) == (qx == 0), out, 0.0)


def split(x):
    high = x.astype(BF16)
    return high, (x - high.astype(F32)).astype(BF16)


def dot3(stacked, high, low):
    rows = stacked.shape[0] // 2
    both = jnp.dot(stacked, high, preferred_element_type=F32)
    rest = jnp.dot(stacked[:rows], low, preferred_element_type=F32)
    return both[:rows] + (both[rows:] + rest)


def send_kernel(info, variants, rec, table, *refs):
    sent, taps = refs[:4], refs[4]
    view, row, col, last = info[0], info[5], info[6], info[7]
    sums = jnp.sum(table[...], axis=-1, keepdims=True)
    taps[...] = table[...] / sums
    for s in range(4):
        q = jnp.bitwise_xor(view, s)
        qx, qy = lax.shift_right_logical(q, 1), jnp.bitwise_and(q, 1)
        rows = pl.ds(pl.multiple_of(112 * qy, 16), 144)
        here = pl.ds(pl.multiple_of(128 * qx, 128), 128)
        there = pl.ds(pl.multiple_of(128 - 128 * qx, 128), 128)
        for z in range(4):
            sent[s][144 * z : 144 * z + 144] = rec[z, rows, here]
        sent[s][576:720] = shared([rec[z, rows, there] for z in range(4)], qx)
        sent[s][720:736] = jnp.zeros((16, 128), F32)
        for n in range(4):
            x = jnp.clip(col + (2 * qx - 1) * (n % 2), 0, GX - 1)
            y = jnp.clip(row + (2 * qy - 1) * (n // 2), 0, last)
            sent[s][720 + 3 * n : 723 + 3 * n, 0:31] = taps[variants[y * GX + x]]


def start_kernel(info, first, main, inside, edge):
    for q in range(4):
        qx, qy = q // 2, q % 2

        @pl.when(info[0] == q)
        def _():
            span = slice(96 * qy, 96 * qy + 160)
            own = [first[z, span, 128 * qx : 128 * qx + 128] for z in range(4)]
            for z in range(4):
                main[z] = own[z]
            beside = [first[z, span, 128 - 128 * qx : 256 - 128 * qx] for z in range(4)]
            inside[...] = packed(beside, 96 * qx, 32)
            edge[...] = packed(own, 96 * qx, 32)


def pack_cols_kernel(info, *refs):
    got, out = refs[:4], refs[4]
    qx = info[1]
    for h in range(2):
        cols = []
        for s in (2 * h, 2 * h + 1):
            block = got[s ^ 2]
            cols.append(shared([block[144 * z : 144 * z + 144] for z in range(4)], qx))
        other = jnp.where(qx == 0, turn(cols[1], 16), turn(cols[1], -16))
        out[h * 144 : h * 144 + 144] = cols[0] + other


def both_sides(inner, cols, odd, qx):
    rows = inner.shape[0]
    if odd:
        cols = jnp.where(qx == 0, turn(cols, 16), turn(cols, -16))
    return jnp.where(right_half(rows) == (qx == 0), inner, cols)


def pack_rows_kernel(info, *refs):
    got, cols, out = refs[:4], refs[4], refs[5]
    at = pl.multiple_of(128 * info[2], 16)
    for s in range(4):
        o = s ^ 1
        for z in range(4):
            n = 4 * s + z
            out[n * 16 : n * 16 + 16] = got[o][pl.ds(144 * z + at, 16)]
        inner = got[o][pl.ds(576 + at, 16)]
        outer = cols[pl.ds((o // 2) * 144 + at, 16)]
        out[256 + 16 * s : 272 + 16 * s] = both_sides(inner, outer, o % 2, info[1])


def start_rows_kernel(info, main, inside, cols, out):
    at = pl.multiple_of(128 * info[2], 32)
    for z in range(4):
        out[32 * z : 32 * z + 32] = main[z, pl.ds(at, 32)]
    out[128:160] = inside[pl.ds(at, 32)]
    out[160:192] = cols[pl.ds(at, 32)]


def toeplitz(base, shift):
    return pltpu.roll(base, shift % 256, axis=1, stride=1, stride_axis=0)


def matrices_kernel(info, one, two, xh, xl, ah, al, y, t, zm, zs):
    qx, qy = info[1], info[2]
    for s, table in enumerate((one, two)):
        fwd = table[720:736]
        flip = lax.broadcasted_iota(jnp.int32, (128, 128), 0) + lanes(128) == 30
        rev = jnp.dot(fwd, flip.astype(F32), precision=lax.Precision.HIGHEST)
        zero = jnp.zeros((16, 128), F32)
        fwd = jnp.concatenate([fwd, zero], 1)
        rev = jnp.concatenate([rev, zero], 1)

        def wide(which, tile, axis, rows):
            return jnp.broadcast_to(which[3 * tile + axis : 3 * tile + axis + 1], (rows, 256))

        lane = lanes(256)
        right, left = lane < 16, (lane >= 16) & (lane < 32)
        for g in range(2):
            near_t = toeplitz(wide(rev, 2 * g, 0, 256), -HALF)
            far_t = toeplitz(wide(rev, 2 * g + 1, 0, 256), -HALF)
            rhs = jnp.where(qx == 1, far_t[:, 128:], near_t[:, 128:])
            lhs = jnp.where(qx == 0, far_t[:, 128:], near_t[:, 128:])
            side = jnp.where(right, rhs, jnp.where(left, turn(lhs, 32), 0.0))
            xh[s, g], xl[s, g] = split(jnp.concatenate([near_t[:, :128], side], 1))
        row = lax.broadcasted_iota(jnp.int32, (256, 256), 0)
        far_row = (row >= 128) & ((row < 192) == (qx == 1))
        base = jnp.where(far_row, wide(fwd, 1, 0, 256), wide(fwd, 0, 0, 256))
        adj = toeplitz(base, -HALF)[:, :128]
        adj = jnp.concatenate(
            [adj[:144], adj[240:], jnp.zeros((96, 128), F32)], 0
        )
        ah[s], al[s] = split(adj)
        for g in range(2):
            row = lax.broadcasted_iota(jnp.int32, (160, 256), 0)
            other = jnp.where(qy == 0, row, 159 - row) < 16
            base = jnp.where(other, wide(fwd, 2 + g, 1, 160), wide(fwd, g, 1, 160))
            y[s, g, :160], y[s, g, 160:] = split(toeplitz(base, 1))
            wider = lanes(128, 256)
            other = jnp.where(qy == 0, wider, 159 - wider) < 16
            near_t = toeplitz(wide(rev, g, 1, 128), 1)
            far_t = toeplitz(wide(rev, 2 + g, 1, 128), 1)
            t[s, g, :128], t[s, g, 128:] = split(jnp.where(other, far_t, near_t))
        lane = lanes(1)
        plane = lax.div(lane, 32)
        far = right_half(1) == (qx == 1)
        for g in range(2):
            near_w = [
                jnp.broadcast_to(fwd[6 * g + 2 : 6 * g + 3, c : c + 1], (1, 128))
                for c in range(12, 19)
            ]
            far_w = [
                jnp.broadcast_to(fwd[6 * g + 5 : 6 * g + 6, c : c + 1], (1, 128))
                for c in range(12, 19)
            ]
            for d in range(7):
                zm[s, g, d : d + 1] = near_w[d]
                inside = (plane + (d - 3) >= 0) & (plane + (d - 3) < 4)
                for adjoint in range(2):
                    c = 6 - d if adjoint else d
                    value = jnp.where(far, far_w[c], near_w[c])
                    at = 8 * adjoint + d
                    zs[s, g, at : at + 1] = jnp.where(inside, value, 0.0)


def sided(left, right, width, n, rows):
    lane = lanes(rows)
    out = jnp.where(lane < width, turn(right, -n * width), 0.0)
    return jnp.where(lane >= 128 - width, turn(left, 128 - width - n * width), out)


def spread(region, e, qx):
    left = jnp.where(qx == 0, region[5], region[4])
    right = jnp.where(qx == 0, region[4], region[5])
    for z in range(4):
        e[0, z, :, :128], e[1, z, :, :128] = split(region[z])
        e[0, z, :, 128:], e[1, z, :, 128:] = split(sided(left, right, 32, z, 192))


def region_kernel(info, main, inside, cols, rows_in, e, region):
    own = pl.multiple_of(32 * (1 - info[2]), 32)
    other = pl.multiple_of(160 * info[2], 32)
    for z in range(4):
        region[z, pl.ds(own, 160)] = main[z]
        region[z, pl.ds(other, 32)] = rows_in[32 * z : 32 * z + 32]
    region[4, pl.ds(own, 160)] = inside[...]
    region[5, pl.ds(own, 160)] = cols[...]
    region[4, pl.ds(other, 32)] = rows_in[128:160]
    region[5, pl.ds(other, 32)] = rows_in[160:192]
    spread(region, e, info[1])


def mix_planes(planes, side, main_w, side_w, adjoint):
    out = []
    for z in range(4):
        order = [3 + z - k if adjoint else 3 + k - z for k in range(4)]
        out.append(sum(main_w[order[k]] * planes[k] for k in range(4)))
    out.append(sum(side_w[d] * turn(side, -32 * (d - 3)) for d in range(7)))
    return out


def forward(s, qy, e, mats, p, put):
    xh, xl, _, _, y, _, zm, zs = mats
    own = pl.multiple_of(32 * (1 - qy), 32)
    other = pl.multiple_of(160 * qy, 32)
    for g, at, count in ((0, own, 160), (1, other, 32)):
        planes, side = [], None
        for z in range(4):
            here = jnp.concatenate([e[0, z, pl.ds(at, count)], e[1, z, pl.ds(at, count)]], 0)
            value = dot3(here, xh[s, g], xl[s, g])
            planes.append(value[:, :128])
            moved = turn(value[:, 128:], 32 * z)
            side = moved if side is None else side + moved
        main_w = [zm[s, g, d : d + 1] for d in range(7)]
        side_w = [zs[s, g, d : d + 1] for d in range(7)]
        for z, value in enumerate(mix_planes(planes, side, main_w, side_w, False)):
            here = slice(128 * z, 128 * z + 128)
            p[0, pl.ds(at, count), here], p[1, pl.ds(at, count), here] = split(value)
    for a in (0, 256):
        put(slice(a, a + 256), dot3(y[s, 0], p[0, :, a : a + 256], p[1, :, a : a + 256]))
    high, low = p[0, :, 512:], p[1, :, 512:]
    near, edge = dot3(y[s, 0], high, low), dot3(y[s, 1], high, low)
    return near, edge


def adjoint(s, mats, r, total):
    _, _, ah, al, _, t, zm, zs = mats
    planes = []
    for a in (0, 256):
        pair = dot3(t[s, 0], r[0, :, a : a + 256], r[1, :, a : a + 256])
        planes += [pair[:, :128], pair[:, 128:]]
    high, low = r[0, :, 512:], r[1, :, 512:]
    return planes, dot3(t[s, 0], high, low), dot3(t[s, 1], high, low)


def finish(s, mats, planes, side, total):
    _, _, ah, al, _, _, zm, zs = mats
    main_w = [zm[s, 0, d : d + 1] for d in range(7)]
    side_w = [zs[s, 0, 8 + d : 9 + d] for d in range(7)]
    *planes, side = mix_planes(planes, side, main_w, side_w, True)
    for z in range(4):
        both = jnp.concatenate([planes[z], turn(side, -32 * z)], 1)
        correction = dot3(jnp.concatenate(split(both), 0), ah[s], al[s])
        total[z] += jnp.log(correction)


def far_mask(rows, qx):
    return right_half(rows) == (qx == 1)


def clear(ref, first):
    ref[:, first:] = jnp.zeros((2, 256 - first, 640), BF16)


def forward_kernel(info, e, *refs):
    mats, refs = refs[:8], refs[8:]
    out, p = refs
    clear(p, 192)
    far = far_mask(160, info[1])

    def body(s, carry):
        def put(where, value):
            out[s, :, where] = value

        near, edge = forward(s, info[2], e, mats, p, put)
        out[s, :, 512:] = jnp.where(far, edge, near)
        return carry

    lax.fori_loop(0, 2, body, 0)


def row_masks(info):
    row = lax.broadcasted_iota(jnp.int32, (160, 128), 0)
    past = jnp.where(info[2] == 0, row, 159 - row) < 16
    inside = (info[4] > 0) | ~past
    side = inside & ((info[3] > 0) | ~far_mask(160, info[1]))
    return inside, side


def take_ratio(s, rec, r, masks, where, blurred):
    wide = jnp.concatenate([masks[0], masks[0]], 1) if blurred.shape[1] == 256 else masks[1]
    ratio = jnp.where(wide, rec[s, :, where] / blurred, 0.0)
    r[0, :160, where], r[1, :160, where] = split(ratio)


def update(first, main, at, total, out, edges, qx):
    new = []
    for z in range(4):
        new.append(main[z, at] * jnp.exp(total[z] / 4))
        out[z] = new[z]
    if first:
        low, high = packed(new, 0, 32), packed(new, 96, 32)
        edges[0][...] = jnp.where(qx == 0, high, low)
        edges[1][...] = jnp.where(qx == 0, low, high)


def adjoint_kernel(info, main, cols, rows_in, *refs):
    got, blurs, refs = refs[:4], refs[4:6], refs[6:]
    groups, refs = (refs[:8], refs[8:16]), refs[16:]
    out, near_edge, far_edge, rec, r, total = refs
    qx, qy = info[1], info[2]
    in_tile = pl.multiple_of(16 * (1 - qy), 16)
    out_tile = pl.multiple_of(144 * qy, 16)
    for s in range(4):
        for z in range(4):
            here = slice(128 * z, 128 * z + 128)
            rec[s, pl.ds(in_tile, 144), here] = got[s][144 * z : 144 * z + 144]
            n = 4 * s + z
            rec[s, pl.ds(out_tile, 16), here] = rows_in[n * 16 : n * 16 + 16]
        outer = cols[(s // 2) * 144 : (s // 2) * 144 + 144]
        rec[s, pl.ds(in_tile, 144), 512:] = both_sides(got[s][576:720], outer, s % 2, qx)
        rec[s, pl.ds(out_tile, 16), 512:] = rows_in[256 + 16 * s : 272 + 16 * s]
    clear(r, 160)
    total[...] = jnp.zeros_like(total)
    masks = row_masks(info)
    far = far_mask(128, qx)
    for pair in range(2):
        mats, blur = groups[pair], blurs[pair]

        def body(s, carry):
            for a, b in ((0, 256), (256, 512), (512, 640)):
                take_ratio(2 * pair + s, rec, r, masks, slice(a, b), blur[s, :, a:b])
            planes, near, edge = adjoint(s, mats, r, total)
            finish(s, mats, planes, jnp.where(far, edge, near), total)
            return carry

        lax.fori_loop(0, 2, body, 0)
    at = pl.ds(pl.multiple_of(32 * qy, 32), 128)
    update(True, main, at, total, out, (near_edge, far_edge), qx)


def step_kernel(info, main, inside, beyond, rows_in, rows_out, rec, *refs):
    groups, refs = (refs[:8], refs[8:16]), refs[16:]
    out, region, e, p, r, total = refs
    qx, qy = info[1], info[2]
    for z in range(4):
        region[z, 32:160] = main[z]
    region[4, 32:160] = inside[...]
    region[5, 32:160] = beyond[...]
    for n in range(6):
        region[n, pl.ds(pl.multiple_of(160 * (1 - qy), 32), 32)] = rows_in[n]
        region[n, pl.ds(pl.multiple_of(160 * qy, 32), 32)] = rows_out[n]
    spread(region, e, qx)
    clear(p, 192)
    clear(r, 160)
    total[...] = jnp.zeros_like(total)
    masks = row_masks(info)
    far160, far128 = far_mask(160, qx), far_mask(128, qx)
    for pair in range(2):
        mats = groups[pair]

        def body(s, carry):
            slot = 2 * pair + s

            def put(where, value):
                take_ratio(slot, rec, r, masks, where, value)

            near, edge = forward(s, qy, e, mats, p, put)
            put(slice(512, 640), jnp.where(far160, edge, near))
            planes, near, edge = adjoint(s, mats, r, total)
            finish(s, mats, planes, jnp.where(far128, edge, near), total)
            return carry

        lax.fori_loop(0, 2, body, 0)
    update(False, main, slice(0, 128), total, out, None, qx)


def per_device(initial, recorded, tap_table, variants):
    tile = lax.axis_index("tile")
    view = lax.axis_index("view")
    count_tiles = lax.axis_size("tile")
    grid_rows = count_tiles // GX
    tile_row, tile_col = tile // GX, tile % GX
    qx, qy = view // 2, view % 2
    has_x = jnp.where(qx == 0, tile_col > 0, tile_col < GX - 1).astype(jnp.int32)
    has_y = jnp.where(qy == 0, tile_row > 0, tile_row < grid_rows - 1).astype(jnp.int32)
    info = jnp.stack([view, qx, qy, has_x, has_y, tile_row, tile_col, grid_rows - 1])

    def route(x, pairs):
        return lax.ppermute(x, ("tile", "view"), pairs)

    def over_view(x, flip):
        return lax.ppermute(x, "view", [(i, i ^ flip) for i in range(4)])

    x_pairs, y_pairs = [], []
    for t in range(count_tiles):
        for v in range(4):
            if v // 2 and t % GX < GX - 1:
                x_pairs += [(4 * t + v, 4 * (t + 1) + v - 2), (4 * (t + 1) + v - 2, 4 * t + v)]
            if v % 2 and t + GX < count_tiles:
                y_pairs += [(4 * t + v, 4 * (t + GX) + v - 1), (4 * (t + GX) + v - 1, 4 * t + v)]

    sent = call(
        send_kernel,
        (shape(736, 128),) * 4,
        [VMEM((8, 3, 31), F32)],
        (info, variants[0]),
        recorded[0, 0],
        tap_table[0],
    )
    got = [sent[0]] + [over_view(sent[s], s) for s in (1, 2, 3)]
    main, inside, edge = call(
        start_kernel,
        (shape(4, 160, 128), shape(160, 128), shape(160, 128)),
        [],
        (info,),
        initial[0],
    )
    start_cols = route(edge, x_pairs)
    start_rows = route(
        call(start_rows_kernel, shape(192, 128), [], (info,), main, inside, start_cols), y_pairs
    )
    e = call(
        region_kernel,
        shape(2, 4, 192, 256, dtype=BF16),
        [VMEM((6, 192, 128), F32)],
        (info,),
        main,
        inside,
        start_cols,
        start_rows,
    )
    mats, blurs = [], []
    for pair in (got[:2], got[2:]):
        mats.append(
            call(
                matrices_kernel,
                (
                    shape(2, 2, 256, 256, dtype=BF16),
                    shape(2, 2, 256, 256, dtype=BF16),
                    shape(2, 256, 128, dtype=BF16),
                    shape(2, 256, 128, dtype=BF16),
                    shape(2, 2, 320, 256, dtype=BF16),
                    shape(2, 2, 256, 256, dtype=BF16),
                    shape(2, 2, 8, 128),
                    shape(2, 2, 16, 128),
                ),
                [],
                (info,),
                *pair,
                flops=1_000_000_000,
            )
        )
        blurs.append(
            call(
                forward_kernel,
                shape(2, 160, 640),
                [VMEM((2, 256, 640), BF16)],
                (info,),
                e,
                *mats[-1],
                flops=2_000_000_000,
            )
        )
    cols = route(call(pack_cols_kernel, shape(288, 128), [], (info,), *got), x_pairs)
    rows = route(call(pack_rows_kernel, shape(320, 128), [], (info,), *got, cols), y_pairs)
    quad = shape(4, 128, 128)
    flat = [*mats[0], *mats[1]]
    estimate, near_edge, far_edge, rec = call(
        adjoint_kernel,
        (quad, shape(128, 128), shape(128, 128), shape(4, 160, 640)),
        [VMEM((2, 256, 640), BF16), VMEM((4, 128, 128), F32)],
        (info,),
        main,
        cols,
        rows,
        *got,
        *blurs,
        *flat,
        flops=4_000_000_000,
    )
    for step in range(1, ITERS):
        inside = over_view(near_edge, 2)
        beyond = route(far_edge, x_pairs)
        whole = jnp.concatenate([estimate, inside[None], beyond[None]])
        low, high = whole[:, :32], whole[:, 96:]
        rows_in = over_view(jnp.where(qy == 0, high, low), 1)
        rows_out = route(jnp.where(qy == 0, low, high), y_pairs)
        estimate = call(
            step_kernel,
            quad,
            [
                VMEM((6, 192, 128), F32),
                VMEM((2, 4, 192, 256), BF16),
                VMEM((2, 256, 640), BF16),
                VMEM((2, 256, 640), BF16),
                VMEM((4, 128, 128), F32),
            ],
            (info,),
            estimate,
            inside,
            beyond,
            rows_in,
            rows_out,
            rec,
            *flat,
            flops=8_000_000_000,
        )
    across = over_view(estimate, 2)
    wide = jnp.where(
        qx == 0,
        jnp.concatenate([estimate, across], 2),
        jnp.concatenate([across, estimate], 2),
    )
    down = over_view(wide, 1)
    return jnp.where(
        qy == 0, jnp.concatenate([wide, down], 1), jnp.concatenate([down, wide], 1)
    )[None]


def solution(mesh):
    return jax.shard_map(
        per_device,
        mesh=mesh,
        in_specs=(
            P("tile", None, None, None),
            P("view", "tile", None, None, None),
            P("view", None, None, None),
            P("view", None),
        ),
        out_specs=P("tile", None, None, None),
        check_vma=False,
    )
```

```python
import functools

import jax
import jax.numpy as jnp
from jax import lax
from jax.experimental import pallas as pl
from jax.experimental.pallas import tpu as pltpu
from jax.sharding import PartitionSpec as P

GX = 8
ITERS = 2
HALF = 15
F32 = jnp.float32
BF16 = jnp.bfloat16
VMEM = pltpu.VMEM
HBM = pltpu.MemorySpace.HBM
SMEM = pltpu.SMEM


def call(body, outs, scratch, scalars, *args, flops=0, in_place=(), in_hbm=(), limit=24):
    specs = [pl.BlockSpec(memory_space=SMEM)] * len(scalars)
    specs += [
        pl.BlockSpec(memory_space=HBM if n in in_place else VMEM) for n in range(len(args))
    ]
    args = [
        pltpu.with_memory_space_constraint(a, HBM) if n in in_place else a
        for n, a in enumerate(args)
    ]
    moved = sum(a.size * a.dtype.itemsize for a in args)
    leaves = [
        HBM(a.shape, a.dtype) if n in in_hbm else a for n, a in enumerate(jax.tree.leaves(outs))
    ]
    return pl.pallas_call(
        body,
        out_shape=jax.tree.unflatten(jax.tree.structure(outs), leaves),
        in_specs=specs,
        out_specs=jax.tree.unflatten(
            jax.tree.structure(outs),
            [
                pl.BlockSpec(memory_space=HBM if n in in_hbm else VMEM)
                for n in range(len(jax.tree.leaves(outs)))
            ],
        ),
        scratch_shapes=scratch,
        compiler_params=pltpu.CompilerParams(vmem_limit_bytes=limit * 1024 * 1024),
        cost_estimate=pl.CostEstimate(flops=flops, bytes_accessed=moved, transcendentals=0),
    )(*scalars, *args)


def shape(*dims, dtype=F32):
    return jax.ShapeDtypeStruct(dims, dtype)


def lanes(rows, width=128):
    return lax.broadcasted_iota(jnp.int32, (rows, width), 1)


def turn(x, amount):
    if isinstance(amount, int):
        amount = amount % x.shape[-1]
        if amount == 0:
            return x
    return pltpu.roll(x, amount, axis=x.ndim - 1)


def packed(pieces, first, width):
    rows = pieces[0].shape[0]
    lane = lanes(rows)
    out = jnp.zeros((rows, 128), F32)
    for n, piece in enumerate(pieces):
        inside = (lane >= n * width) & (lane < (n + 1) * width)
        out = jnp.where(inside, turn(piece, n * width - first), out)
    return out


def right_half(rows):
    return lax.rem(lanes(rows), 32) < 16


def shared(pieces, qx):
    rows = pieces[0].shape[0]
    lane = lanes(rows)
    out = jnp.zeros((rows, 128), F32)
    for z, piece in enumerate(pieces):
        mine = turn(piece, lax.rem(32 * z + 32 * qx, 128))
        out = jnp.where((lane >= 32 * z) & (lane < 32 * z + 32), mine, out)
    return jnp.where(right_half(rows) == (qx == 0), out, 0.0)


def split(x):
    high = x.astype(BF16)
    return high, (x - high.astype(F32)).astype(BF16)


def dot3(stacked, high, low):
    rows = stacked.shape[0] // 2
    both = jnp.dot(stacked, high, preferred_element_type=F32)
    rest = jnp.dot(stacked[:rows], low, preferred_element_type=F32)
    return both[:rows] + (both[rows:] + rest)


def send_kernel(grid_rows, rec, table, variants, *refs):
    sent, (raw, ids, whole, sems) = refs[:4], refs[4:]
    loads = [pltpu.make_async_copy(rec.at[z], whole.at[z], sems.at[z]) for z in range(4)]
    small = [
        pltpu.make_async_copy(table, raw, sems.at[4]),
        pltpu.make_async_copy(variants, ids, sems.at[5]),
    ]
    for load in (*small, *loads):
        load.start()
    tile, view = lax.axis_index("tile"), lax.axis_index("view")
    row, col = lax.div(tile, GX), lax.rem(tile, GX)
    places = []
    for s in range(4):
        q = jnp.bitwise_xor(view, s)
        qx, qy = lax.shift_right_logical(q, 1), jnp.bitwise_and(q, 1)
        rows = pl.ds(pl.multiple_of(112 * qy, 16), 144)
        here = pl.ds(pl.multiple_of(128 * qx, 128), 128)
        there = pl.ds(pl.multiple_of(128 - 128 * qx, 128), 128)
        places.append((qx, qy, rows, here, there))
    for load in small:
        load.wait()
    raw[...] = raw[...] / jnp.sum(raw[...], axis=-1, keepdims=True)
    for s, (qx, qy, _, _, _) in enumerate(places):
        sent[s][648:664] = jnp.zeros((16, 128), F32)
        for n in range(4):
            x = jnp.clip(col + (2 * qx - 1) * (n % 2), 0, GX - 1)
            y = jnp.clip(row + (2 * qy - 1) * (n // 2), 0, grid_rows - 1)
            which = ids[0, y * GX + x]
            for axis in range(3):
                at = 648 + 3 * n + axis
                sent[s][at : at + 1, 0:31] = raw[axis, pl.ds(which, 1)]
    for z in range(4):
        loads[z].wait()
        for s, (_, _, rows, here, _) in enumerate(places):
            sent[s][144 * z : 144 * z + 144] = whole[z, rows, here]
    for s, (qx, _, rows, _, there) in enumerate(places):
        side = shared([whole[z, rows, there] for z in range(4)], qx)
        sent[s][576:648] = side[:72] + turn(side[72:], 16 + 96 * qx)


def own_side(block, qx):
    side = block[576:648]
    mine = right_half(72) == (qx == 0)
    low = jnp.where(mine, turn(side, 112 - 96 * qx), 0.0)
    return jnp.concatenate([jnp.where(mine, side, 0.0), low], 0)


def start_kernel(first, main, inside, edge):
    view = lax.axis_index("view")
    for q in range(4):
        qx, qy = q // 2, q % 2

        @pl.when(view == q)
        def _():
            span = slice(96 * qy, 96 * qy + 160)
            own = [first[z, span, 128 * qx : 128 * qx + 128] for z in range(4)]
            for z in range(4):
                main[z] = own[z]
            beside = [first[z, span, 128 - 128 * qx : 256 - 128 * qx] for z in range(4)]
            inside[...] = packed(beside, 96 * qx, 32)
            edge[...] = packed(own, 96 * qx, 32)


def pack_cols_kernel(info, *refs):
    got, out = refs[:4], refs[4]
    qx = info[1]
    for h in range(2):
        cols = []
        for s in (2 * h, 2 * h + 1):
            block = got[s ^ 2]
            cols.append(shared([block[144 * z : 144 * z + 144] for z in range(4)], qx))
        other = turn(cols[1], 16 + 96 * qx)
        out[h * 144 : h * 144 + 144] = cols[0] + other


def both_sides(inner, cols, odd, qx):
    rows = inner.shape[0]
    if odd:
        cols = turn(cols, 16 + 96 * qx)
    return jnp.where(right_half(rows) == (qx == 0), inner, cols)


def pack_rows_kernel(info, *refs):
    got, cols, out = refs[:4], refs[4], refs[5]
    at = pl.multiple_of(128 * info[2], 16)
    sides = [own_side(got[s], info[1]) for s in range(4)]
    for s in range(4):
        o = s ^ 1
        for z in range(4):
            n = 4 * s + z
            out[n * 16 : n * 16 + 16] = got[o][pl.ds(144 * z + at, 16)]
        inner = jnp.where(info[2] == 0, sides[o][:16], sides[o][128:])
        outer = cols[pl.ds((o // 2) * 144 + at, 16)]
        out[256 + 16 * s : 272 + 16 * s] = both_sides(inner, outer, o % 2, info[1])


def start_rows_kernel(info, main, inside, cols, out):
    at = pl.multiple_of(128 * info[2], 32)
    for z in range(4):
        out[32 * z : 32 * z + 32] = main[z, pl.ds(at, 32)]
    out[128:160] = inside[pl.ds(at, 32)]
    out[160:192] = jnp.where(info[3] > 0, cols[pl.ds(at, 32)], 0.0)


def toeplitz(base, shift):
    return pltpu.roll(base, shift % 256, axis=1, stride=1, stride_axis=0)


def matrices_kernel(info, one, two, xh, xl, ah, al, y, t, zm, zs):
    qx, qy = info[1], info[2]
    for s, table in enumerate((one, two)):
        fwd = table[648:664]
        flip = lax.broadcasted_iota(jnp.int32, (128, 128), 0) + lanes(128) == 30
        rev = jnp.dot(fwd, flip.astype(F32), precision=lax.Precision.HIGHEST)
        zero = jnp.zeros((16, 128), F32)
        fwd = jnp.concatenate([fwd, zero], 1)
        rev = jnp.concatenate([rev, zero], 1)

        def wide(which, tile, axis, rows):
            return jnp.broadcast_to(which[3 * tile + axis : 3 * tile + axis + 1], (rows, 256))

        lane = lanes(256)
        right, left = lane < 16, (lane >= 16) & (lane < 32)
        for g in range(2):
            near_t = toeplitz(wide(rev, 2 * g, 0, 256), -HALF)
            far_t = toeplitz(wide(rev, 2 * g + 1, 0, 256), -HALF)
            rhs = jnp.where(qx == 1, far_t[:, 128:], near_t[:, 128:])
            lhs = jnp.where(qx == 0, far_t[:, 128:], near_t[:, 128:])
            side = jnp.where(right, rhs, jnp.where(left, turn(lhs, 32), 0.0))
            xh[s, g], xl[s, g] = split(jnp.concatenate([near_t[:, :128], side], 1))
        row = lax.broadcasted_iota(jnp.int32, (256, 256), 0)
        far_row = (row >= 128) & ((row < 192) == (qx == 1))
        base = jnp.where(far_row, wide(fwd, 1, 0, 256), wide(fwd, 0, 0, 256))
        adj = toeplitz(base, -HALF)[:, :128]
        adj = jnp.concatenate(
            [adj[:144], adj[240:], jnp.zeros((96, 128), F32)], 0
        )
        ah[s], al[s] = split(adj)
        for g in range(2):
            row = lax.broadcasted_iota(jnp.int32, (160, 256), 0)
            other = jnp.where(qy == 0, row, 159 - row) < 16
            base = jnp.where(other, wide(fwd, 2 + g, 1, 160), wide(fwd, g, 1, 160))
            y[s, g, :160], y[s, g, 160:] = split(toeplitz(base, 1))
            wider = lanes(128, 256)
            other = jnp.where(qy == 0, wider, 159 - wider) < 16
            near_t = toeplitz(wide(rev, g, 1, 128), 1)
            far_t = toeplitz(wide(rev, 2 + g, 1, 128), 1)
            t[s, g, :128], t[s, g, 128:] = split(jnp.where(other, far_t, near_t))
        lane = lanes(1)
        plane = lax.div(lane, 32)
        far = right_half(1) == (qx == 1)
        for g in range(2):
            near_w = [
                jnp.broadcast_to(fwd[6 * g + 2 : 6 * g + 3, c : c + 1], (1, 128))
                for c in range(12, 19)
            ]
            far_w = [
                jnp.broadcast_to(fwd[6 * g + 5 : 6 * g + 6, c : c + 1], (1, 128))
                for c in range(12, 19)
            ]
            for d in range(7):
                zm[s, g, d : d + 1] = near_w[d]
                inside = (plane + (d - 3) >= 0) & (plane + (d - 3) < 4)
                for adjoint in range(2):
                    c = 6 - d if adjoint else d
                    value = jnp.where(far, far_w[c], near_w[c])
                    at = 8 * adjoint + d
                    zs[s, g, at : at + 1] = jnp.where(inside, value, 0.0)


def sided(left, right, width, n, rows):
    lane = lanes(rows)
    out = jnp.where(lane < width, turn(right, -n * width), 0.0)
    return jnp.where(lane >= 128 - width, turn(left, 128 - width - n * width), out)


def spread(region, e, qx):
    left = jnp.where(qx == 0, region[5], region[4])
    right = jnp.where(qx == 0, region[4], region[5])
    for z in range(4):
        e[0, z, :, :128], e[1, z, :, :128] = split(region[z])
        e[0, z, :, 128:], e[1, z, :, 128:] = split(sided(left, right, 32, z, 192))


def region_kernel(info, main, inside, cols, rows_in, e, region):
    own = pl.multiple_of(32 * (1 - info[2]), 32)
    other = pl.multiple_of(160 * info[2], 32)
    for z in range(4):
        region[z, pl.ds(own, 160)] = main[z]
    for n in range(6):
        region[n, pl.ds(other, 32)] = jnp.where(
            info[4] > 0, rows_in[32 * n : 32 * n + 32], 0.0
        )
    region[4, pl.ds(own, 160)] = inside[...]
    region[5, pl.ds(own, 160)] = jnp.where(info[3] > 0, cols[...], 0.0)
    spread(region, e, info[1])


def mix_planes(planes, side, main_w, side_w, adjoint):
    out = []
    for z in range(4):
        order = [3 + z - k if adjoint else 3 + k - z for k in range(4)]
        out.append(sum(main_w[order[k]] * planes[k] for k in range(4)))
    out.append(sum(side_w[d] * turn(side, -32 * (d - 3)) for d in range(7)))
    return out


def forward(s, qy, e, mats, p, put):
    xh, xl, _, _, y, _, zm, zs = mats
    own = pl.multiple_of(32 * (1 - qy), 32)
    other = pl.multiple_of(160 * qy, 32)
    for g, at, count in ((0, own, 160), (1, other, 32)):
        planes, side = [], None
        for z in range(4):
            here = jnp.concatenate([e[0, z, pl.ds(at, count)], e[1, z, pl.ds(at, count)]], 0)
            value = dot3(here, xh[s, g], xl[s, g])
            planes.append(value[:, :128])
            moved = turn(value[:, 128:], 32 * z)
            side = moved if side is None else side + moved
        main_w = [zm[s, g, d : d + 1] for d in range(7)]
        side_w = [zs[s, g, d : d + 1] for d in range(7)]
        for z, value in enumerate(mix_planes(planes, side, main_w, side_w, False)):
            here = slice(128 * z, 128 * z + 128)
            p[0, pl.ds(at, count), here], p[1, pl.ds(at, count), here] = split(value)
    for a in (0, 256):
        put(slice(a, a + 256), dot3(y[s, 0], p[0, :, a : a + 256], p[1, :, a : a + 256]))
    high, low = p[0, :, 512:], p[1, :, 512:]
    near, edge = dot3(y[s, 0], high, low), dot3(y[s, 1], high, low)
    return near, edge


def adjoint(s, mats, r, total):
    _, _, ah, al, _, t, zm, zs = mats
    planes = []
    for a in (0, 256):
        pair = dot3(t[s, 0], r[0, :, a : a + 256], r[1, :, a : a + 256])
        planes += [pair[:, :128], pair[:, 128:]]
    high, low = r[0, :, 512:], r[1, :, 512:]
    return planes, dot3(t[s, 0], high, low), dot3(t[s, 1], high, low)


def finish(s, mats, planes, side, total):
    _, _, ah, al, _, _, zm, zs = mats
    main_w = [zm[s, 0, d : d + 1] for d in range(7)]
    side_w = [zs[s, 0, 8 + d : 9 + d] for d in range(7)]
    *planes, side = mix_planes(planes, side, main_w, side_w, True)
    for z in range(4):
        both = jnp.concatenate([planes[z], turn(side, -32 * z)], 1)
        correction = dot3(jnp.concatenate(split(both), 0), ah[s], al[s])
        total[z] += jnp.log(correction)


def far_mask(rows, qx):
    return right_half(rows) == (qx == 1)


def clear(ref, first):
    ref[:, first:] = jnp.zeros((2, 256 - first, 640), BF16)


def forward_kernel(info, e, *refs):
    mats, refs = refs[:8], refs[8:]
    out, p = refs
    clear(p, 192)
    far = far_mask(160, info[1])

    def body(s, carry):
        def put(where, value):
            out[s, :, where] = value

        near, edge = forward(s, info[2], e, mats, p, put)
        out[s, :, 512:] = jnp.where(far, edge, near)
        return carry

    lax.fori_loop(0, 2, body, 0)


def row_masks(info):
    row = lax.broadcasted_iota(jnp.int32, (160, 128), 0)
    past = jnp.where(info[2] == 0, row, 159 - row) < 16
    inside = (info[4] > 0) | ~past
    side = inside & ((info[3] > 0) | ~far_mask(160, info[1]))
    return inside, side


def take_ratio(s, rec, r, masks, where, blurred):
    wide = jnp.concatenate([masks[0], masks[0]], 1) if blurred.shape[1] == 256 else masks[1]
    ratio = jnp.where(wide, rec[s, :, where] / blurred, 0.0)
    r[0, :160, where], r[1, :160, where] = split(ratio)


def update(first, main, at, total, out, edges, qx):
    new = []
    for z in range(4):
        new.append(main[z, at] * jnp.exp(total[z] / 4))
        out[z] = new[z]
    if first:
        low, high = packed(new, 0, 32), packed(new, 96, 32)
        edges[0][...] = jnp.where(qx == 0, high, low)
        edges[1][...] = jnp.where(qx == 0, low, high)


def adjoint_kernel(info, main, cols, rows_in, *refs):
    got, blurs, refs = refs[:4], refs[4:6], refs[6:]
    groups, refs = (refs[:8], refs[8:16]), refs[16:]
    out, near_edge, far_edge, kept, rec, r, total, sem = refs
    qx, qy = info[1], info[2]
    in_tile = pl.multiple_of(16 * (1 - qy), 16)
    out_tile = pl.multiple_of(144 * qy, 16)
    for s in range(4):
        for z in range(4):
            here = slice(128 * z, 128 * z + 128)
            rec[s, pl.ds(in_tile, 144), here] = got[s][144 * z : 144 * z + 144]
            n = 4 * s + z
            rec[s, pl.ds(out_tile, 16), here] = rows_in[n * 16 : n * 16 + 16]
        outer = cols[(s // 2) * 144 : (s // 2) * 144 + 144]
        rec[s, pl.ds(in_tile, 144), 512:] = both_sides(own_side(got[s], qx), outer, s % 2, qx)
        rec[s, pl.ds(out_tile, 16), 512:] = rows_in[256 + 16 * s : 272 + 16 * s]
    keep = pltpu.make_async_copy(rec, kept, sem)
    keep.start()
    clear(r, 160)
    total[...] = jnp.zeros_like(total)
    masks = row_masks(info)
    far = far_mask(128, qx)
    for pair in range(2):
        mats, blur = groups[pair], blurs[pair]

        def body(s, carry):
            for a, b in ((0, 256), (256, 512), (512, 640)):
                take_ratio(2 * pair + s, rec, r, masks, slice(a, b), blur[s, :, a:b])
            planes, near, edge = adjoint(s, mats, r, total)
            finish(s, mats, planes, jnp.where(far, edge, near), total)
            return carry

        lax.fori_loop(0, 2, body, 0)
    at = pl.ds(pl.multiple_of(32 * qy, 32), 128)
    update(True, main, at, total, out, (near_edge, far_edge), qx)
    keep.wait()


def step_kernel(info, main, inside, beyond, rows_in, rows_out, *refs):
    far_refs, (out, region, e, p, r, total), refs = refs[:17], refs[17:23], refs[23:]
    near_refs, sems = refs[:17], refs[17]
    loads = []
    for n, (there, here) in enumerate(zip(far_refs, near_refs, strict=True)):
        loads.append(pltpu.make_async_copy(there, here, sems.at[n]))
    for n in (0, 1, 4, 6, 7, 8, 5, 2, 3, 9, 10, 13, 15, 16, 14, 11, 12):
        loads[n].start()
    groups, rec = (near_refs[:8], near_refs[9:]), near_refs[8]
    qx, qy = info[1], info[2]
    for z in range(4):
        region[z, 32:160] = main[z]
    region[4, 32:160] = inside[...]
    region[5, 32:160] = jnp.where(info[3] > 0, beyond[...], 0.0)
    for n in range(6):
        region[n, pl.ds(pl.multiple_of(160 * (1 - qy), 32), 32)] = rows_in[n]
        region[n, pl.ds(pl.multiple_of(160 * qy, 32), 32)] = jnp.where(
            info[4] > 0, rows_out[n], 0.0
        )
    spread(region, e, qx)
    clear(p, 192)
    clear(r, 160)
    total[...] = jnp.zeros_like(total)
    masks = row_masks(info)
    far160, far128 = far_mask(160, qx), far_mask(128, qx)
    for pair in range(2):
        mats = groups[pair]
        early, late = ((0, 1, 4, 6, 7), (8, 5, 2, 3)) if pair == 0 else ((9, 10, 13, 15, 16), (14, 11, 12))
        for n in early:
            loads[n].wait()

        def body(s, carry):
            slot = 2 * pair + s

            def put(where, value):
                if where.start == 0:

                    @pl.when(s == 0)
                    def _():
                        for n in late:
                            loads[n].wait()

                take_ratio(slot, rec, r, masks, where, value)

            near, edge = forward(s, qy, e, mats, p, put)
            put(slice(512, 640), jnp.where(far160, edge, near))
            planes, near, edge = adjoint(s, mats, r, total)
            finish(s, mats, planes, jnp.where(far128, edge, near), total)
            return carry

        lax.fori_loop(0, 2, body, 0)
    update(False, main, slice(0, 128), total, out, None, qx)


def make_matrices(info, one, two):
    return call(
        matrices_kernel,
        (
            shape(2, 2, 256, 256, dtype=BF16),
            shape(2, 2, 256, 256, dtype=BF16),
            shape(2, 256, 128, dtype=BF16),
            shape(2, 256, 128, dtype=BF16),
            shape(2, 2, 320, 256, dtype=BF16),
            shape(2, 2, 256, 256, dtype=BF16),
            shape(2, 2, 8, 128),
            shape(2, 2, 16, 128),
        ),
        [],
        (info,),
        one,
        two,
        flops=1_000_000_000,
    )


def per_device(initial, recorded, tap_table, variants):
    tile = lax.axis_index("tile")
    view = lax.axis_index("view")
    count_tiles = lax.axis_size("tile")
    grid_rows = count_tiles // GX
    tile_row, tile_col = tile // GX, tile % GX
    qx, qy = view // 2, view % 2
    has_x = jnp.where(qx == 0, tile_col > 0, tile_col < GX - 1).astype(jnp.int32)
    has_y = jnp.where(qy == 0, tile_row > 0, tile_row < grid_rows - 1).astype(jnp.int32)
    info = jnp.stack([view, qx, qy, has_x, has_y])

    def route(x, pairs):
        return lax.ppermute(x, ("tile", "view"), pairs)

    def over_view(x, flip):
        return lax.ppermute(x, "view", [(i, i ^ flip) for i in range(4)])

    x_pairs, y_pairs = [], []
    for t in range(count_tiles):
        for v in range(4):
            me, right, below = 4 * t + v, 4 * (t + 1) + v - 2, 4 * (t + GX) + v - 1
            if v // 2 and t % GX < GX - 1:
                x_pairs += [(me, right), (right, me)]
            if v % 2 and t + GX < count_tiles:
                y_pairs += [(me, below), (below, me)]
            if t % GX == (GX - 1 if v // 2 else 0):
                x_pairs.append((me, 4 * t + (v ^ 1)))
            if t // GX == (grid_rows - 1 if v % 2 else 0):
                y_pairs.append((me, 4 * t + (v ^ 2)))

    sent = call(
        functools.partial(send_kernel, grid_rows),
        (shape(664, 128),) * 4,
        [
            VMEM((3, 8, 31), F32),
            SMEM((1, count_tiles), jnp.int32),
            VMEM((4, 256, 256), F32),
            pltpu.SemaphoreType.DMA((6,)),
        ],
        (),
        recorded[0, 0],
        tap_table[0].transpose(1, 0, 2),
        variants,
        in_place=(0, 1, 2),
    )
    got = [sent[0]] + [over_view(sent[s], s) for s in (1, 2, 3)]
    main, inside, edge = call(
        start_kernel,
        (shape(4, 160, 128), shape(160, 128), shape(160, 128)),
        [],
        (),
        initial[0],
    )
    start_cols = route(edge, x_pairs)
    mats = [make_matrices(info, *got[:2])]
    start_cols, mats[0] = lax.optimization_barrier((start_cols, mats[0]))
    start_rows = route(
        call(start_rows_kernel, shape(192, 128), [], (info,), main, inside, start_cols), y_pairs
    )
    e = call(
        region_kernel,
        shape(2, 4, 192, 256, dtype=BF16),
        [VMEM((6, 192, 128), F32)],
        (info,),
        main,
        inside,
        start_cols,
        start_rows,
    )
    e, got = lax.optimization_barrier((e, got))
    mats.append(make_matrices(info, *got[2:]))
    blurs = [
        call(
            forward_kernel,
            shape(2, 160, 640),
            [VMEM((2, 256, 640), BF16)],
            (info,),
            e,
            *group,
            flops=2_000_000_000,
        )
        for group in mats
    ]
    cols = route(call(pack_cols_kernel, shape(288, 128), [], (info,), *got), x_pairs)
    rows = route(call(pack_rows_kernel, shape(320, 128), [], (info,), *got, cols), y_pairs)
    quad = shape(4, 128, 128)
    flat = [*mats[0], *mats[1]]
    estimate, near_edge, far_edge, rec = call(
        adjoint_kernel,
        (quad, shape(128, 128), shape(128, 128), shape(4, 160, 640)),
        [
            VMEM((4, 160, 640), F32),
            VMEM((2, 256, 640), BF16),
            VMEM((4, 128, 128), F32),
            pltpu.SemaphoreType.DMA,
        ],
        (info,),
        main,
        cols,
        rows,
        *got,
        *blurs,
        *flat,
        flops=4_000_000_000,
        in_hbm=(3,),
    )
    for step in range(1, ITERS):
        inside = over_view(near_edge, 2)
        beyond = route(far_edge, x_pairs)
        shown = jnp.where(has_x > 0, beyond, 0.0)
        whole = jnp.concatenate([estimate, inside[None], shown[None]])
        low, high = whole[:, :32], whole[:, 96:]
        rows_in = over_view(jnp.where(qy == 0, high, low), 1)
        rows_out = route(jnp.where(qy == 0, low, high), y_pairs)
        far_args = [*mats[0], rec, *mats[1]]
        estimate = call(
            step_kernel,
            quad,
            [
                VMEM((6, 192, 128), F32),
                VMEM((2, 4, 192, 256), BF16),
                VMEM((2, 256, 640), BF16),
                VMEM((2, 256, 640), BF16),
                VMEM((4, 128, 128), F32),
                *(VMEM(a.shape, a.dtype) for a in far_args),
                pltpu.SemaphoreType.DMA((17,)),
            ],
            (info,),
            estimate,
            inside,
            beyond,
            rows_in,
            rows_out,
            *far_args,
            flops=8_000_000_000,
            in_place=range(5, 22),
        )
    across, down = over_view(estimate, 2), over_view(estimate, 1)
    corner = over_view(across, 1)
    halves = []
    for y in range(2):
        near, far = jnp.where(qy == y, estimate, down), jnp.where(qy == y, across, corner)
        left, right = jnp.where(qx == 0, near, far), jnp.where(qx == 0, far, near)
        halves.append(jnp.concatenate([left, right], 2))
    return jnp.concatenate(halves, 1)[None]


def solution(mesh):
    return jax.shard_map(
        per_device,
        mesh=mesh,
        in_specs=(
            P("tile", None, None, None),
            P("view", "tile", None, None, None),
            P("view", None, None, None),
            P("view", None),
        ),
        out_specs=P("tile", None, None, None),
        check_vma=False,
    )
```

```python
import functools

import jax
import jax.numpy as jnp
from jax import lax
from jax.experimental import pallas as pl
from jax.experimental.pallas import tpu as pltpu
from jax.sharding import PartitionSpec as P

GX = 8
ITERS = 2
HALF = 15
F32 = jnp.float32
BF16 = jnp.bfloat16
VMEM = pltpu.VMEM
HBM = pltpu.MemorySpace.HBM
SMEM = pltpu.SMEM


def position():
    tile, view = lax.axis_index("tile"), lax.axis_index("view")
    qx, qy = lax.shift_right_logical(view, 1), jnp.bitwise_and(view, 1)
    col, row = lax.rem(tile, GX), lax.div(tile, GX)
    last = lax.axis_size("tile") // GX - 1
    has_x = jnp.where(qx == 0, col, GX - 1 - col)
    has_y = jnp.where(qy == 0, row, last - row)
    return view, qx, qy, has_x, has_y


def call(body, outs, scratch, *args, flops=0, in_place=(), kept_in=(), kept_out=(), limit=24):
    specs = [
        pl.BlockSpec(memory_space=HBM if n in in_place else VMEM) for n in range(len(args))
    ]
    args = list(args)
    for n in in_place:
        args[n] = pltpu.with_memory_space_constraint(args[n], HBM)
    for n in kept_in:
        args[n] = pltpu.with_memory_space_constraint(args[n], VMEM)
    moved = sum(a.size * a.dtype.itemsize for a in args)
    leaves = [
        VMEM(a.shape, a.dtype) if n in kept_out else a for n, a in enumerate(jax.tree.leaves(outs))
    ]
    return pl.pallas_call(
        lambda *refs: body(position(), *refs),
        out_shape=jax.tree.unflatten(jax.tree.structure(outs), leaves),
        in_specs=specs,
        out_specs=jax.tree.map(lambda _: pl.BlockSpec(memory_space=VMEM), outs),
        scratch_shapes=scratch,
        compiler_params=pltpu.CompilerParams(vmem_limit_bytes=limit * 1024 * 1024),
        cost_estimate=pl.CostEstimate(flops=flops, bytes_accessed=moved, transcendentals=0),
    )(*args)


def shape(*dims, dtype=F32):
    return jax.ShapeDtypeStruct(dims, dtype)


def lanes(rows, width=128):
    return lax.broadcasted_iota(jnp.int32, (rows, width), 1)


def turn(x, amount):
    if isinstance(amount, int):
        amount = amount % x.shape[-1]
        if amount == 0:
            return x
    return pltpu.roll(x, amount, axis=x.ndim - 1)


def packed(pieces, first, width):
    rows = pieces[0].shape[0]
    lane = lanes(rows)
    out = jnp.zeros((rows, 128), F32)
    for n, piece in enumerate(pieces):
        inside = (lane >= n * width) & (lane < (n + 1) * width)
        out = jnp.where(inside, turn(piece, n * width - first), out)
    return out


def right_half(rows):
    return lax.rem(lanes(rows), 32) < 16


def shared(pieces, qx):
    rows = pieces[0].shape[0]
    lane = lanes(rows)
    out = jnp.zeros((rows, 128), F32)
    for z, piece in enumerate(pieces):
        mine = turn(piece, lax.rem(32 * z + 32 * qx, 128))
        out = jnp.where((lane >= 32 * z) & (lane < 32 * z + 32), mine, out)
    return jnp.where(right_half(rows) == (qx == 0), out, 0.0)


def split(x):
    high = x.astype(BF16)
    return high, (x - high.astype(F32)).astype(BF16)


def dot3(stacked, high, low):
    rows = stacked.shape[0] // 2
    both = jnp.dot(stacked, high, preferred_element_type=F32)
    rest = jnp.dot(stacked[:rows], low, preferred_element_type=F32)
    return both[:rows] + (both[rows:] + rest)


def send_kernel(grid_rows, info, rec, table, variants, *refs):
    sent, (raw, ids, whole, sems) = refs[:4], refs[4:]
    loads = [pltpu.make_async_copy(rec.at[z], whole.at[z], sems.at[z]) for z in range(4)]
    small = [
        pltpu.make_async_copy(table, raw, sems.at[4]),
        pltpu.make_async_copy(variants, ids, sems.at[5]),
    ]
    for load in (*small, *loads):
        load.start()
    tile, view = lax.axis_index("tile"), lax.axis_index("view")
    row, col = lax.div(tile, GX), lax.rem(tile, GX)
    places = []
    for s in range(4):
        q = jnp.bitwise_xor(view, s)
        qx, qy = lax.shift_right_logical(q, 1), jnp.bitwise_and(q, 1)
        rows = pl.ds(pl.multiple_of(112 * qy, 16), 144)
        here = pl.ds(pl.multiple_of(128 * qx, 128), 128)
        there = pl.ds(pl.multiple_of(128 - 128 * qx, 128), 128)
        places.append((qx, qy, rows, here, there))
    for load in small:
        load.wait()
    raw[...] = raw[...] / jnp.sum(raw[...], axis=-1, keepdims=True)
    for s, (qx, qy, _, _, _) in enumerate(places):
        sent[s][648:664] = jnp.zeros((16, 128), F32)
        for n in range(4):
            x = jnp.clip(col + (2 * qx - 1) * (n % 2), 0, GX - 1)
            y = jnp.clip(row + (2 * qy - 1) * (n // 2), 0, grid_rows - 1)
            which = ids[0, y * GX + x]
            for axis in range(3):
                at = 648 + 3 * n + axis
                sent[s][at : at + 1, 0:31] = raw[axis, pl.ds(which, 1)]
    for z in range(4):
        loads[z].wait()
        for s, (_, _, rows, here, _) in enumerate(places):
            sent[s][144 * z : 144 * z + 144] = whole[z, rows, here]
    for s, (qx, _, rows, _, there) in enumerate(places):
        side = shared([whole[z, rows, there] for z in range(4)], qx)
        sent[s][576:648] = side[:72] + turn(side[72:], 16 + 96 * qx)


def own_side(block, qx):
    side = block[576:648]
    mine = right_half(72) == (qx == 0)
    low = jnp.where(mine, turn(side, 112 - 96 * qx), 0.0)
    return jnp.concatenate([jnp.where(mine, side, 0.0), low], 0)


def start_kernel(info, first, main, inside, edge):
    view = info[0]
    for q in range(4):
        qx, qy = q // 2, q % 2

        @pl.when(view == q)
        def _():
            span = slice(96 * qy, 96 * qy + 160)
            own = [first[z, span, 128 * qx : 128 * qx + 128] for z in range(4)]
            for z in range(4):
                main[z] = own[z]
            beside = [first[z, span, 128 - 128 * qx : 256 - 128 * qx] for z in range(4)]
            inside[...] = packed(beside, 96 * qx, 32)
            edge[...] = packed(own, 96 * qx, 32)


def pack_cols_kernel(info, *refs):
    got, out = refs[:4], refs[4]
    qx = info[1]
    for h in range(2):
        cols = []
        for s in (2 * h, 2 * h + 1):
            block = got[s ^ 2]
            cols.append(shared([block[144 * z : 144 * z + 144] for z in range(4)], qx))
        other = turn(cols[1], 16 + 96 * qx)
        out[h * 144 : h * 144 + 144] = cols[0] + other


def both_sides(inner, cols, odd, qx):
    rows = inner.shape[0]
    if odd:
        cols = turn(cols, 16 + 96 * qx)
    return jnp.where(right_half(rows) == (qx == 0), inner, cols)


def pack_rows_kernel(info, *refs):
    got, cols, out = refs[:4], refs[4], refs[5]
    at = pl.multiple_of(128 * info[2], 16)
    sides = [own_side(got[s], info[1]) for s in range(4)]
    for s in range(4):
        o = s ^ 1
        for z in range(4):
            n = 4 * s + z
            out[n * 16 : n * 16 + 16] = got[o][pl.ds(144 * z + at, 16)]
        inner = jnp.where(info[2] == 0, sides[o][:16], sides[o][128:])
        outer = cols[pl.ds((o // 2) * 144 + at, 16)]
        out[256 + 16 * s : 272 + 16 * s] = both_sides(inner, outer, o % 2, info[1])


def start_rows_kernel(info, main, inside, cols, out):
    at = pl.multiple_of(128 * info[2], 32)
    for z in range(4):
        out[32 * z : 32 * z + 32] = main[z, pl.ds(at, 32)]
    out[128:160] = inside[pl.ds(at, 32)]
    out[160:192] = jnp.where(info[3] > 0, cols[pl.ds(at, 32)], 0.0)


def toeplitz(base, shift):
    return pltpu.roll(base, shift % 256, axis=1, stride=1, stride_axis=0)


def matrices_kernel(info, one, two, xh, xl, ah, al, y, t, zm, zs):
    qx, qy = info[1], info[2]
    for s, table in enumerate((one, two)):
        fwd = table[648:664]
        flip = lax.broadcasted_iota(jnp.int32, (128, 128), 0) + lanes(128) == 30
        rev = jnp.dot(fwd, flip.astype(F32), precision=lax.Precision.HIGHEST)
        zero = jnp.zeros((16, 128), F32)
        fwd = jnp.concatenate([fwd, zero], 1)
        rev = jnp.concatenate([rev, zero], 1)

        def wide(which, tile, axis, rows):
            return jnp.broadcast_to(which[3 * tile + axis : 3 * tile + axis + 1], (rows, 256))

        lane = lanes(256)
        right, left = lane < 16, (lane >= 16) & (lane < 32)
        for g in range(2):
            near_t = toeplitz(wide(rev, 2 * g, 0, 256), -HALF)
            far_t = toeplitz(wide(rev, 2 * g + 1, 0, 256), -HALF)
            rhs = jnp.where(qx == 1, far_t[:, 128:], near_t[:, 128:])
            lhs = jnp.where(qx == 0, far_t[:, 128:], near_t[:, 128:])
            side = jnp.where(right, rhs, jnp.where(left, turn(lhs, 32), 0.0))
            xh[s, g], xl[s, g] = split(jnp.concatenate([near_t[:, :128], side], 1))
        row = lax.broadcasted_iota(jnp.int32, (256, 256), 0)
        far_row = (row >= 128) & ((row < 192) == (qx == 1))
        base = jnp.where(far_row, wide(fwd, 1, 0, 256), wide(fwd, 0, 0, 256))
        adj = toeplitz(base, -HALF)[:, :128]
        adj = jnp.concatenate(
            [adj[:144], adj[240:], jnp.zeros((96, 128), F32)], 0
        )
        ah[s], al[s] = split(adj)
        for g in range(2):
            row = lax.broadcasted_iota(jnp.int32, (160, 256), 0)
            other = jnp.where(qy == 0, row, 159 - row) < 16
            base = jnp.where(other, wide(fwd, 2 + g, 1, 160), wide(fwd, g, 1, 160))
            y[s, g, :160], y[s, g, 160:] = split(toeplitz(base, 1))
            wider = lanes(128, 256)
            other = jnp.where(qy == 0, wider, 159 - wider) < 16
            near_t = toeplitz(wide(rev, g, 1, 128), 1)
            far_t = toeplitz(wide(rev, 2 + g, 1, 128), 1)
            t[s, g, :128], t[s, g, 128:] = split(jnp.where(other, far_t, near_t))
        lane = lanes(1)
        plane = lax.div(lane, 32)
        far = right_half(1) == (qx == 1)
        for g in range(2):
            near_w = [
                jnp.broadcast_to(fwd[6 * g + 2 : 6 * g + 3, c : c + 1], (1, 128))
                for c in range(12, 19)
            ]
            far_w = [
                jnp.broadcast_to(fwd[6 * g + 5 : 6 * g + 6, c : c + 1], (1, 128))
                for c in range(12, 19)
            ]
            for d in range(7):
                zm[s, g, d : d + 1] = near_w[d]
                inside = (plane + (d - 3) >= 0) & (plane + (d - 3) < 4)
                for adjoint in range(2):
                    c = 6 - d if adjoint else d
                    value = jnp.where(far, far_w[c], near_w[c])
                    at = 8 * adjoint + d
                    zs[s, g, at : at + 1] = jnp.where(inside, value, 0.0)


def sided(left, right, width, n, rows):
    lane = lanes(rows)
    out = jnp.where(lane < width, turn(right, -n * width), 0.0)
    return jnp.where(lane >= 128 - width, turn(left, 128 - width - n * width), out)


def spread(region, e, qx):
    left = jnp.where(qx == 0, region[5], region[4])
    right = jnp.where(qx == 0, region[4], region[5])
    for z in range(4):
        e[0, z, :, :128], e[1, z, :, :128] = split(region[z])
        e[0, z, :, 128:], e[1, z, :, 128:] = split(sided(left, right, 32, z, 192))


def region_kernel(info, main, inside, cols, rows_in, e, region):
    own = pl.multiple_of(32 * (1 - info[2]), 32)
    other = pl.multiple_of(160 * info[2], 32)
    for z in range(4):
        region[z, pl.ds(own, 160)] = main[z]
    for n in range(6):
        region[n, pl.ds(other, 32)] = jnp.where(
            info[4] > 0, rows_in[32 * n : 32 * n + 32], 0.0
        )
    region[4, pl.ds(own, 160)] = inside[...]
    region[5, pl.ds(own, 160)] = jnp.where(info[3] > 0, cols[...], 0.0)
    spread(region, e, info[1])


def mix_planes(planes, side, main_w, side_w, adjoint):
    out = []
    for z in range(4):
        order = [3 + z - k if adjoint else 3 + k - z for k in range(4)]
        out.append(sum(main_w[order[k]] * planes[k] for k in range(4)))
    out.append(sum(side_w[d] * turn(side, -32 * (d - 3)) for d in range(7)))
    return out


def forward(s, qy, e, mats, p, put):
    xh, xl, _, _, y, _, zm, zs = mats
    own = pl.multiple_of(32 * (1 - qy), 32)
    other = pl.multiple_of(160 * qy, 32)
    for g, at, count in ((0, own, 160), (1, other, 32)):
        planes, side = [], None
        for z in range(4):
            here = jnp.concatenate([e[0, z, pl.ds(at, count)], e[1, z, pl.ds(at, count)]], 0)
            value = dot3(here, xh[s, g], xl[s, g])
            planes.append(value[:, :128])
            moved = turn(value[:, 128:], 32 * z)
            side = moved if side is None else side + moved
        main_w = [zm[s, g, d : d + 1] for d in range(7)]
        side_w = [zs[s, g, d : d + 1] for d in range(7)]
        for z, value in enumerate(mix_planes(planes, side, main_w, side_w, False)):
            here = slice(128 * z, 128 * z + 128)
            p[0, pl.ds(at, count), here], p[1, pl.ds(at, count), here] = split(value)
    for a in (0, 256):
        put(slice(a, a + 256), dot3(y[s, 0], p[0, :, a : a + 256], p[1, :, a : a + 256]))
    high, low = p[0, :, 512:], p[1, :, 512:]
    near, edge = dot3(y[s, 0], high, low), dot3(y[s, 1], high, low)
    return near, edge


def adjoint(s, mats, r, total):
    _, _, ah, al, _, t, zm, zs = mats
    planes = []
    for a in (0, 256):
        pair = dot3(t[s, 0], r[0, :, a : a + 256], r[1, :, a : a + 256])
        planes += [pair[:, :128], pair[:, 128:]]
    high, low = r[0, :, 512:], r[1, :, 512:]
    return planes, dot3(t[s, 0], high, low), dot3(t[s, 1], high, low)


def finish(s, mats, planes, side, total):
    _, _, ah, al, _, _, zm, zs = mats
    main_w = [zm[s, 0, d : d + 1] for d in range(7)]
    side_w = [zs[s, 0, 8 + d : 9 + d] for d in range(7)]
    *planes, side = mix_planes(planes, side, main_w, side_w, True)
    for z in range(4):
        both = jnp.concatenate([planes[z], turn(side, -32 * z)], 1)
        correction = dot3(jnp.concatenate(split(both), 0), ah[s], al[s])
        total[z] += jnp.log(correction)


def far_mask(rows, qx):
    return right_half(rows) == (qx == 1)


def clear(ref, first):
    ref[:, first:] = jnp.zeros((2, 256 - first, 640), BF16)


def forward_kernel(info, e, *refs):
    mats, refs = refs[:8], refs[8:]
    out, p = refs
    far = far_mask(160, info[1])
    for s in range(2):
        clear(p.at[s], 192)

        def put(where, value):
            out[s, :, where] = value

        near, edge = forward(s, info[2], e, mats, p.at[s], put)
        out[s, :, 512:] = jnp.where(far, edge, near)


def row_masks(info):
    row = lax.broadcasted_iota(jnp.int32, (160, 128), 0)
    past = jnp.where(info[2] == 0, row, 159 - row) < 16
    inside = (info[4] > 0) | ~past
    side = inside & ((info[3] > 0) | ~far_mask(160, info[1]))
    return inside, side


def take_ratio(s, rec, r, masks, where, blurred):
    wide = jnp.concatenate([masks[0], masks[0]], 1) if blurred.shape[1] == 256 else masks[1]
    ratio = jnp.where(wide, rec[s, :, where] / blurred, 0.0)
    r[0, :160, where], r[1, :160, where] = split(ratio)


def update(first, main, at, total, out, edges, qx):
    new = []
    for z in range(4):
        new.append(main[z, at] * jnp.exp(total[z] / 4))
        out[z] = new[z]
    if first:
        low, high = packed(new, 0, 32), packed(new, 96, 32)
        edges[0][...] = jnp.where(qx == 0, high, low)
        edges[1][...] = jnp.where(qx == 0, low, high)


def adjoint_kernel(info, main, cols, rows_in, *refs):
    got, blurs, refs = refs[:4], refs[4:6], refs[6:]
    groups, refs = (refs[:8], refs[8:16]), refs[16:]
    out, near_edge, far_edge, rec, r, total = refs
    qx, qy = info[1], info[2]
    in_tile = pl.multiple_of(16 * (1 - qy), 16)
    out_tile = pl.multiple_of(144 * qy, 16)
    for s in range(4):
        for z in range(4):
            here = slice(128 * z, 128 * z + 128)
            rec[s, pl.ds(in_tile, 144), here] = got[s][144 * z : 144 * z + 144]
            n = 4 * s + z
            rec[s, pl.ds(out_tile, 16), here] = rows_in[n * 16 : n * 16 + 16]
        outer = cols[(s // 2) * 144 : (s // 2) * 144 + 144]
        rec[s, pl.ds(in_tile, 144), 512:] = both_sides(own_side(got[s], qx), outer, s % 2, qx)
        rec[s, pl.ds(out_tile, 16), 512:] = rows_in[256 + 16 * s : 272 + 16 * s]
    for s in range(2):
        clear(r.at[s], 160)
    total[...] = jnp.zeros_like(total)
    masks = row_masks(info)
    far = far_mask(128, qx)
    for pair in range(2):
        mats, blur = groups[pair], blurs[pair]

        for s in range(2):
            for a, b in ((0, 256), (256, 512), (512, 640)):
                take_ratio(2 * pair + s, rec, r.at[s], masks, slice(a, b), blur[s, :, a:b])
            planes, near, edge = adjoint(s, mats, r.at[s], total)
            finish(s, mats, planes, jnp.where(far, edge, near), total)
    at = pl.ds(pl.multiple_of(32 * qy, 32), 128)
    update(True, main, at, total, out, (near_edge, far_edge), qx)


def mid_rows_kernel(info, main, inside, beyond, near, far):
    shown = (
        *(main.at[z] for z in range(4)),
        inside,
        beyond,
    )
    for out, at in ((near, 96 - 96 * info[2]), (far, 96 * info[2])):
        rows = pl.ds(pl.multiple_of(at, 32), 32)
        for n in range(6):
            piece = shown[n][rows]
            out[n] = jnp.where(info[3] > 0, piece, 0.0) if n == 5 else piece


def step_kernel(info, main, inside, beyond, rows_in, rows_out, *refs):
    rec, groups, refs = refs[0], (refs[1:9], refs[9:17]), refs[17:]
    out, region, e, p, r, total = refs
    qx, qy = info[1], info[2]
    for z in range(4):
        region[z, 32:160] = main[z]
    region[4, 32:160] = inside[...]
    region[5, 32:160] = jnp.where(info[3] > 0, beyond[...], 0.0)
    for n in range(6):
        region[n, pl.ds(pl.multiple_of(160 * (1 - qy), 32), 32)] = rows_in[n]
        region[n, pl.ds(pl.multiple_of(160 * qy, 32), 32)] = jnp.where(
            info[4] > 0, rows_out[n], 0.0
        )
    spread(region, e, qx)
    for s in range(2):
        clear(p.at[s], 192)
        clear(r.at[s], 160)
    total[...] = jnp.zeros_like(total)
    masks = row_masks(info)
    far160, far128 = far_mask(160, qx), far_mask(128, qx)
    for pair in range(2):
        mats = groups[pair]
        for s in range(2):
            slot = 2 * pair + s

            def put(where, value):
                take_ratio(slot, rec, r.at[s], masks, where, value)

            near, edge = forward(s, qy, e, mats, p.at[s], put)
            put(slice(512, 640), jnp.where(far160, edge, near))
            planes, near, edge = adjoint(s, mats, r.at[s], total)
            finish(s, mats, planes, jnp.where(far128, edge, near), total)
    update(False, main, slice(0, 128), total, out, None, qx)


def make_matrices(one, two):
    return call(
        matrices_kernel,
        (
            shape(2, 2, 256, 256, dtype=BF16),
            shape(2, 2, 256, 256, dtype=BF16),
            shape(2, 256, 128, dtype=BF16),
            shape(2, 256, 128, dtype=BF16),
            shape(2, 2, 320, 256, dtype=BF16),
            shape(2, 2, 256, 256, dtype=BF16),
            shape(2, 2, 8, 128),
            shape(2, 2, 16, 128),
        ),
        [],
        one,
        two,
        flops=1_000_000_000,
        kept_out=range(8),
    )


def per_device(initial, recorded, tap_table, variants):
    count_tiles = lax.axis_size("tile")
    grid_rows = count_tiles // GX

    def route(x, pairs):
        return lax.ppermute(x, ("tile", "view"), pairs)

    def over_view(x, flip):
        return lax.ppermute(x, "view", [(i, i ^ flip) for i in range(4)])

    x_pairs, y_pairs = [], []
    for t in range(count_tiles):
        for v in range(4):
            me, right, below = 4 * t + v, 4 * (t + 1) + v - 2, 4 * (t + GX) + v - 1
            if v // 2 and t % GX < GX - 1:
                x_pairs += [(me, right), (right, me)]
            if v % 2 and t + GX < count_tiles:
                y_pairs += [(me, below), (below, me)]
            if t % GX == (GX - 1 if v // 2 else 0):
                x_pairs.append((me, 4 * t + (v ^ 1)))
            if t // GX == (grid_rows - 1 if v % 2 else 0):
                y_pairs.append((me, 4 * t + (v ^ 2)))

    sent = call(
        functools.partial(send_kernel, grid_rows),
        (shape(664, 128),) * 4,
        [
            VMEM((3, 8, 31), F32),
            SMEM((1, count_tiles), jnp.int32),
            VMEM((4, 256, 256), F32),
            pltpu.SemaphoreType.DMA((6,)),
        ],
        recorded[0, 0],
        tap_table[0].transpose(1, 0, 2),
        variants,
        in_place=(0, 1, 2),
    )
    got = [sent[0]] + [over_view(sent[s], s) for s in (1, 2, 3)]
    main, inside, edge = call(
        start_kernel,
        (shape(4, 160, 128), shape(160, 128), shape(160, 128)),
        [],
        initial[0],
    )
    start_cols = route(edge, x_pairs)
    mats = [make_matrices(*got[:2])]
    start_cols, mats[0] = lax.optimization_barrier((start_cols, mats[0]))
    start_rows = route(
        call(start_rows_kernel, shape(192, 128), [], main, inside, start_cols), y_pairs
    )
    e = call(
        region_kernel,
        shape(2, 4, 192, 256, dtype=BF16),
        [VMEM((6, 192, 128), F32)],
        main,
        inside,
        start_cols,
        start_rows,
    )
    e, got = lax.optimization_barrier((e, got))
    mats.append(make_matrices(*got[2:]))
    blurs = [
        call(
            forward_kernel,
            shape(2, 160, 640),
            [VMEM((2, 2, 256, 640), BF16)],
                e,
            *group,
            flops=2_000_000_000,
            kept_in=range(1, 9),
        )
        for group in mats
    ]
    cols = route(call(pack_cols_kernel, shape(288, 128), [], *got), x_pairs)
    rows = route(call(pack_rows_kernel, shape(320, 128), [], *got, cols), y_pairs)
    quad = shape(4, 128, 128)
    flat = [*mats[0], *mats[1]]
    estimate, near_edge, far_edge, rec = call(
        adjoint_kernel,
        (quad, shape(128, 128), shape(128, 128), shape(4, 160, 640)),
        [
            VMEM((2, 2, 256, 640), BF16),
            VMEM((4, 128, 128), F32),
        ],
        main,
        cols,
        rows,
        *got,
        *blurs,
        *flat,
        flops=4_000_000_000,
        kept_in=range(9, 25),
        kept_out=(3,),
    )
    for step in range(1, ITERS):
        inside = over_view(near_edge, 2)
        beyond = route(far_edge, x_pairs)
        near, far = call(
            mid_rows_kernel, (shape(6, 32, 128),) * 2, [], estimate, inside, beyond
        )
        rows_in = over_view(near, 1)
        rows_out = route(far, y_pairs)
        estimate = call(
            step_kernel,
            quad,
            [
                VMEM((6, 192, 128), F32),
                VMEM((2, 4, 192, 256), BF16),
                VMEM((2, 2, 256, 640), BF16),
                VMEM((2, 2, 256, 640), BF16),
                VMEM((4, 128, 128), F32),
            ],
                estimate,
            inside,
            beyond,
            rows_in,
            rows_out,
            rec,
            *flat,
            flops=8_000_000_000,
            kept_in=range(5, 22),
        )
    view = lax.axis_index("view")
    qx, qy = view // 2, view % 2
    across, down = over_view(estimate, 2), over_view(estimate, 1)
    corner = over_view(across, 1)
    halves = []
    for y in range(2):
        near, far = jnp.where(qy == y, estimate, down), jnp.where(qy == y, across, corner)
        left, right = jnp.where(qx == 0, near, far), jnp.where(qx == 0, far, near)
        halves.append(jnp.concatenate([left, right], 2))
    return jnp.concatenate(halves, 1)[None]


def solution(mesh):
    return jax.shard_map(
        per_device,
        mesh=mesh,
        in_specs=(
            P("tile", None, None, None),
            P("view", "tile", None, None, None),
            P("view", None, None, None),
            P("view", None),
        ),
        out_specs=P("tile", None, None, None),
        check_vma=False,
    )
```

```python
import functools

import jax
import jax.numpy as jnp
from jax import lax
from jax.experimental import pallas as pl
from jax.experimental.pallas import tpu as pltpu
from jax.sharding import PartitionSpec as P

GX = 8
ITERS = 2
HALF = 15
F32 = jnp.float32
BF16 = jnp.bfloat16
VMEM = pltpu.VMEM
HBM = pltpu.MemorySpace.HBM
SMEM = pltpu.SMEM


def position():
    tile, view = lax.axis_index("tile"), lax.axis_index("view")
    qx, qy = lax.shift_right_logical(view, 1), jnp.bitwise_and(view, 1)
    col, row = lax.rem(tile, GX), lax.div(tile, GX)
    last = lax.axis_size("tile") // GX - 1
    has_x = jnp.where(qx == 0, col, GX - 1 - col)
    has_y = jnp.where(qy == 0, row, last - row)
    return view, qx, qy, has_x, has_y


def call(body, outs, scratch, *args, flops=0, in_place=(), kept_in=(), kept_out=(), after=None, limit=24):
    specs = [
        pl.BlockSpec(memory_space=HBM if n in in_place else VMEM) for n in range(len(args))
    ]
    args = list(args)
    for n in in_place:
        args[n] = pltpu.with_memory_space_constraint(args[n], HBM)
    for n in kept_in:
        args[n] = pltpu.with_memory_space_constraint(args[n], VMEM)
    plain = body
    if after is not None:
        specs.append(pl.BlockSpec(memory_space=pl.ANY))
        args.append(after)

        def body(info, *refs):
            plain(info, *refs[: len(args) - 1], *refs[len(args) :])

    moved = sum(a.size * a.dtype.itemsize for a in args)
    leaves = [
        VMEM(a.shape, a.dtype) if n in kept_out else a for n, a in enumerate(jax.tree.leaves(outs))
    ]
    return pl.pallas_call(
        lambda *refs: body(position(), *refs),
        out_shape=jax.tree.unflatten(jax.tree.structure(outs), leaves),
        in_specs=specs,
        out_specs=jax.tree.map(lambda _: pl.BlockSpec(memory_space=VMEM), outs),
        scratch_shapes=scratch,
        compiler_params=pltpu.CompilerParams(vmem_limit_bytes=limit * 1024 * 1024),
        cost_estimate=pl.CostEstimate(flops=flops, bytes_accessed=moved, transcendentals=0),
    )(*args)


def shape(*dims, dtype=F32):
    return jax.ShapeDtypeStruct(dims, dtype)


def lanes(rows, width=128):
    return lax.broadcasted_iota(jnp.int32, (rows, width), 1)


def turn(x, amount):
    if isinstance(amount, int):
        amount = amount % x.shape[-1]
        if amount == 0:
            return x
    return pltpu.roll(x, amount, axis=x.ndim - 1)


def packed(pieces, first, width):
    rows = pieces[0].shape[0]
    lane = lanes(rows)
    out = jnp.zeros((rows, 128), F32)
    for n, piece in enumerate(pieces):
        inside = (lane >= n * width) & (lane < (n + 1) * width)
        out = jnp.where(inside, turn(piece, n * width - first), out)
    return out


def right_half(rows):
    return lax.rem(lanes(rows), 32) < 16


def shared(pieces, qx):
    rows = pieces[0].shape[0]
    lane = lanes(rows)
    out = jnp.zeros((rows, 128), F32)
    for z, piece in enumerate(pieces):
        mine = turn(piece, lax.rem(32 * z + 32 * qx, 128))
        out = jnp.where((lane >= 32 * z) & (lane < 32 * z + 32), mine, out)
    return jnp.where(right_half(rows) == (qx == 0), out, 0.0)


def split(x):
    high = x.astype(BF16)
    return high, (x - high.astype(F32)).astype(BF16)


def dot3(stacked, high, low):
    rows = stacked.shape[0] // 2
    both = jnp.dot(stacked, high, preferred_element_type=F32)
    rest = jnp.dot(stacked[:rows], low, preferred_element_type=F32)
    return both[:rows] + (both[rows:] + rest)


def send_kernel(grid_rows, info, rec, table, variants, *refs):
    sent, (raw, ids, whole, sems) = refs[:4], refs[4:]
    loads = [pltpu.make_async_copy(rec.at[z], whole.at[z], sems.at[z]) for z in range(4)]
    small = [
        pltpu.make_async_copy(table, raw, sems.at[4]),
        pltpu.make_async_copy(variants, ids, sems.at[5]),
    ]
    for load in (*small, *loads):
        load.start()
    tile, view = lax.axis_index("tile"), lax.axis_index("view")
    row, col = lax.div(tile, GX), lax.rem(tile, GX)
    places = []
    for s in range(4):
        q = jnp.bitwise_xor(view, s)
        qx, qy = lax.shift_right_logical(q, 1), jnp.bitwise_and(q, 1)
        rows = pl.ds(pl.multiple_of(112 * qy, 16), 144)
        here = pl.ds(pl.multiple_of(128 * qx, 128), 128)
        there = pl.ds(pl.multiple_of(128 - 128 * qx, 128), 128)
        places.append((qx, qy, rows, here, there))
    for load in small:
        load.wait()
    raw[...] = raw[...] / jnp.sum(raw[...], axis=-1, keepdims=True)
    for s, (qx, qy, _, _, _) in enumerate(places):
        sent[s][648:664] = jnp.zeros((16, 128), F32)
        for n in range(4):
            x = jnp.clip(col + (2 * qx - 1) * (n % 2), 0, GX - 1)
            y = jnp.clip(row + (2 * qy - 1) * (n // 2), 0, grid_rows - 1)
            which = ids[0, y * GX + x]
            for axis in range(3):
                at = 648 + 3 * n + axis
                sent[s][at : at + 1, 0:31] = raw[axis, pl.ds(which, 1)]
    for z in range(4):
        loads[z].wait()
        for s, (_, _, rows, here, _) in enumerate(places):
            sent[s][144 * z : 144 * z + 144] = whole[z, rows, here]
    for s, (qx, _, rows, _, there) in enumerate(places):
        side = shared([whole[z, rows, there] for z in range(4)], qx)
        sent[s][576:648] = side[:72] + turn(side[72:], 16 + 96 * qx)


def own_side(block, qx):
    side = block[576:648]
    mine = right_half(72) == (qx == 0)
    low = jnp.where(mine, turn(side, 112 - 96 * qx), 0.0)
    return jnp.concatenate([jnp.where(mine, side, 0.0), low], 0)


def start_kernel(info, first, main, inside, edge):
    view = info[0]
    for q in range(4):
        qx, qy = q // 2, q % 2

        @pl.when(view == q)
        def _():
            span = slice(96 * qy, 96 * qy + 160)
            own = [first[z, span, 128 * qx : 128 * qx + 128] for z in range(4)]
            for z in range(4):
                main[z] = own[z]
            beside = [first[z, span, 128 - 128 * qx : 256 - 128 * qx] for z in range(4)]
            inside[...] = packed(beside, 96 * qx, 32)
            edge[...] = packed(own, 96 * qx, 32)


def pack_cols_kernel(info, *refs):
    got, out = refs[:4], refs[4]
    qx = info[1]
    for h in range(2):
        cols = []
        for s in (2 * h, 2 * h + 1):
            block = got[s ^ 2]
            cols.append(shared([block[144 * z : 144 * z + 144] for z in range(4)], qx))
        other = turn(cols[1], 16 + 96 * qx)
        out[h * 144 : h * 144 + 144] = cols[0] + other


def both_sides(inner, cols, odd, qx):
    rows = inner.shape[0]
    if odd:
        cols = turn(cols, 16 + 96 * qx)
    return jnp.where(right_half(rows) == (qx == 0), inner, cols)


def pack_rows_kernel(info, *refs):
    got, cols, out = refs[:4], refs[4], refs[5]
    at = pl.multiple_of(128 * info[2], 16)
    sides = [own_side(got[s], info[1]) for s in range(4)]
    for s in range(4):
        o = s ^ 1
        for z in range(4):
            n = 4 * s + z
            out[n * 16 : n * 16 + 16] = got[o][pl.ds(144 * z + at, 16)]
        inner = jnp.where(info[2] == 0, sides[o][:16], sides[o][128:])
        outer = cols[pl.ds((o // 2) * 144 + at, 16)]
        out[256 + 16 * s : 272 + 16 * s] = both_sides(inner, outer, o % 2, info[1])


def start_rows_kernel(info, main, inside, cols, out):
    at = pl.multiple_of(128 * info[2], 32)
    for z in range(4):
        out[32 * z : 32 * z + 32] = main[z, pl.ds(at, 32)]
    out[128:160] = inside[pl.ds(at, 32)]
    out[160:192] = jnp.where(info[3] > 0, cols[pl.ds(at, 32)], 0.0)


def toeplitz(base, shift):
    return pltpu.roll(base, shift % 256, axis=1, stride=1, stride_axis=0)


def matrices_kernel(info, one, two, xh, xl, ah, al, y, t, zm, zs):
    qx, qy = info[1], info[2]
    for s, table in enumerate((one, two)):
        fwd = table[648:664]
        flip = lax.broadcasted_iota(jnp.int32, (128, 128), 0) + lanes(128) == 30
        rev = jnp.dot(fwd, flip.astype(F32), precision=lax.Precision.HIGHEST)
        zero = jnp.zeros((16, 128), F32)
        fwd = jnp.concatenate([fwd, zero], 1)
        rev = jnp.concatenate([rev, zero], 1)

        def wide(which, tile, axis, rows):
            return jnp.broadcast_to(which[3 * tile + axis : 3 * tile + axis + 1], (rows, 256))

        lane = lanes(256)
        right, left = lane < 16, (lane >= 16) & (lane < 32)
        for g in range(2):
            near_t = toeplitz(wide(rev, 2 * g, 0, 256), -HALF)
            far_t = toeplitz(wide(rev, 2 * g + 1, 0, 256), -HALF)
            rhs = jnp.where(qx == 1, far_t[:, 128:], near_t[:, 128:])
            lhs = jnp.where(qx == 0, far_t[:, 128:], near_t[:, 128:])
            side = jnp.where(right, rhs, jnp.where(left, turn(lhs, 32), 0.0))
            xh[s, g], xl[s, g] = split(jnp.concatenate([near_t[:, :128], side], 1))
        row = lax.broadcasted_iota(jnp.int32, (256, 256), 0)
        far_row = (row >= 128) & ((row < 192) == (qx == 1))
        base = jnp.where(far_row, wide(fwd, 1, 0, 256), wide(fwd, 0, 0, 256))
        adj = toeplitz(base, -HALF)[:, :128]
        adj = jnp.concatenate(
            [adj[:144], adj[240:], jnp.zeros((96, 128), F32)], 0
        )
        ah[s], al[s] = split(adj)
        for g in range(2):
            row = lax.broadcasted_iota(jnp.int32, (160, 256), 0)
            other = jnp.where(qy == 0, row, 159 - row) < 16
            base = jnp.where(other, wide(fwd, 2 + g, 1, 160), wide(fwd, g, 1, 160))
            y[s, g, :160], y[s, g, 160:] = split(toeplitz(base, 1))
            wider = lanes(128, 256)
            other = jnp.where(qy == 0, wider, 159 - wider) < 16
            near_t = toeplitz(wide(rev, g, 1, 128), 1)
            far_t = toeplitz(wide(rev, 2 + g, 1, 128), 1)
            t[s, g, :128], t[s, g, 128:] = split(jnp.where(other, far_t, near_t))
        lane = lanes(1)
        plane = lax.div(lane, 32)
        far = right_half(1) == (qx == 1)
        for g in range(2):
            near_w = [
                jnp.broadcast_to(fwd[6 * g + 2 : 6 * g + 3, c : c + 1], (1, 128))
                for c in range(12, 19)
            ]
            far_w = [
                jnp.broadcast_to(fwd[6 * g + 5 : 6 * g + 6, c : c + 1], (1, 128))
                for c in range(12, 19)
            ]
            for d in range(7):
                zm[s, g, d : d + 1] = near_w[d]
                inside = (plane + (d - 3) >= 0) & (plane + (d - 3) < 4)
                for adjoint in range(2):
                    c = 6 - d if adjoint else d
                    value = jnp.where(far, far_w[c], near_w[c])
                    at = 8 * adjoint + d
                    zs[s, g, at : at + 1] = jnp.where(inside, value, 0.0)


def sided(left, right, width, n, rows):
    lane = lanes(rows)
    out = jnp.where(lane < width, turn(right, -n * width), 0.0)
    return jnp.where(lane >= 128 - width, turn(left, 128 - width - n * width), out)


def spread(region, e, qx):
    left = jnp.where(qx == 0, region[5], region[4])
    right = jnp.where(qx == 0, region[4], region[5])
    for z in range(4):
        e[0, z, :, :128], e[1, z, :, :128] = split(region[z])
        e[0, z, :, 128:], e[1, z, :, 128:] = split(sided(left, right, 32, z, 192))


def region_kernel(info, main, inside, cols, rows_in, e, region):
    own = pl.multiple_of(32 * (1 - info[2]), 32)
    other = pl.multiple_of(160 * info[2], 32)
    for z in range(4):
        region[z, pl.ds(own, 160)] = main[z]
    for n in range(6):
        region[n, pl.ds(other, 32)] = jnp.where(
            info[4] > 0, rows_in[32 * n : 32 * n + 32], 0.0
        )
    region[4, pl.ds(own, 160)] = inside[...]
    region[5, pl.ds(own, 160)] = jnp.where(info[3] > 0, cols[...], 0.0)
    spread(region, e, info[1])


def mix_planes(planes, side, main_w, side_w, adjoint):
    out = []
    for z in range(4):
        order = [3 + z - k if adjoint else 3 + k - z for k in range(4)]
        out.append(sum(main_w[order[k]] * planes[k] for k in range(4)))
    out.append(sum(side_w[d] * turn(side, -32 * (d - 3)) for d in range(7)))
    return out


def forward(s, qy, e, mats, p, put):
    xh, xl, _, _, y, _, zm, zs = mats
    own = pl.multiple_of(32 * (1 - qy), 32)
    other = pl.multiple_of(160 * qy, 32)
    for g, at, count in ((0, own, 160), (1, other, 32)):
        planes, side = [], None
        for z in range(4):
            here = jnp.concatenate([e[0, z, pl.ds(at, count)], e[1, z, pl.ds(at, count)]], 0)
            value = dot3(here, xh[s, g], xl[s, g])
            planes.append(value[:, :128])
            moved = turn(value[:, 128:], 32 * z)
            side = moved if side is None else side + moved
        main_w = [zm[s, g, d : d + 1] for d in range(7)]
        side_w = [zs[s, g, d : d + 1] for d in range(7)]
        for z, value in enumerate(mix_planes(planes, side, main_w, side_w, False)):
            here = slice(128 * z, 128 * z + 128)
            p[0, pl.ds(at, count), here], p[1, pl.ds(at, count), here] = split(value)
    for a in (0, 256):
        put(slice(a, a + 256), dot3(y[s, 0], p[0, :, a : a + 256], p[1, :, a : a + 256]))
    high, low = p[0, :, 512:], p[1, :, 512:]
    near, edge = dot3(y[s, 0], high, low), dot3(y[s, 1], high, low)
    return near, edge


def adjoint(s, mats, r, total):
    _, _, ah, al, _, t, zm, zs = mats
    planes = []
    for a in (0, 256):
        pair = dot3(t[s, 0], r[0, :, a : a + 256], r[1, :, a : a + 256])
        planes += [pair[:, :128], pair[:, 128:]]
    high, low = r[0, :, 512:], r[1, :, 512:]
    return planes, dot3(t[s, 0], high, low), dot3(t[s, 1], high, low)


def finish(s, mats, planes, side, total):
    _, _, ah, al, _, _, zm, zs = mats
    main_w = [zm[s, 0, d : d + 1] for d in range(7)]
    side_w = [zs[s, 0, 8 + d : 9 + d] for d in range(7)]
    *planes, side = mix_planes(planes, side, main_w, side_w, True)
    for z in range(4):
        both = jnp.concatenate([planes[z], turn(side, -32 * z)], 1)
        correction = dot3(jnp.concatenate(split(both), 0), ah[s], al[s])
        total[z] += jnp.log(correction)


def far_mask(rows, qx):
    return right_half(rows) == (qx == 1)


def clear(ref, first):
    ref[:, first:] = jnp.zeros((2, 256 - first, 640), BF16)


def forward_kernel(parts, info, e, *refs):
    groups, (out, p) = (refs[:8], refs[8:-2]), refs[-2:]
    far = far_mask(160, info[1])
    for n, (group, s) in enumerate(parts):
        clear(p.at[n], 192)

        def put(where, value):
            out[n, :, where] = value

        near, edge = forward(s, info[2], e, groups[group], p.at[n], put)
        out[n, :, 512:] = jnp.where(far, edge, near)


def row_masks(info):
    row = lax.broadcasted_iota(jnp.int32, (160, 128), 0)
    past = jnp.where(info[2] == 0, row, 159 - row) < 16
    inside = (info[4] > 0) | ~past
    side = inside & ((info[3] > 0) | ~far_mask(160, info[1]))
    return inside, side


def take_ratio(s, rec, r, masks, where, blurred):
    wide = jnp.concatenate([masks[0], masks[0]], 1) if blurred.shape[1] == 256 else masks[1]
    ratio = jnp.where(wide, rec[s, :, where] / blurred, 0.0)
    r[0, :160, where], r[1, :160, where] = split(ratio)


def update(first, main, at, total, out, edges, qx):
    new = []
    for z in range(4):
        new.append(main[z, at] * jnp.exp(total[z] / 4))
        out[z] = new[z]
    if first:
        low, high = packed(new, 0, 32), packed(new, 96, 32)
        edges[0][...] = jnp.where(qx == 0, high, low)
        edges[1][...] = jnp.where(qx == 0, low, high)


def adjoint_kernel(info, main, cols, rows_in, *refs):
    got, blurs, refs = refs[:4], refs[4:6], refs[6:]
    groups, refs = (refs[:8], refs[8:16]), refs[16:]
    out, near_edge, far_edge, rec, r, total = refs
    qx, qy = info[1], info[2]
    in_tile = pl.multiple_of(16 * (1 - qy), 16)
    out_tile = pl.multiple_of(144 * qy, 16)
    for s in range(4):
        for z in range(4):
            here = slice(128 * z, 128 * z + 128)
            rec[s, pl.ds(in_tile, 144), here] = got[s][144 * z : 144 * z + 144]
            n = 4 * s + z
            rec[s, pl.ds(out_tile, 16), here] = rows_in[n * 16 : n * 16 + 16]
        outer = cols[(s // 2) * 144 : (s // 2) * 144 + 144]
        rec[s, pl.ds(in_tile, 144), 512:] = both_sides(own_side(got[s], qx), outer, s % 2, qx)
        rec[s, pl.ds(out_tile, 16), 512:] = rows_in[256 + 16 * s : 272 + 16 * s]
    for s in range(2):
        clear(r.at[s], 160)
    total[...] = jnp.zeros_like(total)
    masks = row_masks(info)
    far = far_mask(128, qx)
    for pair in range(2):
        mats = groups[pair]

        for s in range(2):
            for a, b in ((0, 256), (256, 512), (512, 640)):
                slot = 2 * pair + s
                blurred = blurs[1][slot - 1, :, a:b] if slot else blurs[0][0, :, a:b]
                take_ratio(slot, rec, r.at[s], masks, slice(a, b), blurred)
            planes, near, edge = adjoint(s, mats, r.at[s], total)
            finish(s, mats, planes, jnp.where(far, edge, near), total)
    at = pl.ds(pl.multiple_of(32 * qy, 32), 128)
    update(True, main, at, total, out, (near_edge, far_edge), qx)


def mid_rows_kernel(info, main, inside, beyond, near, far):
    shown = (
        *(main.at[z] for z in range(4)),
        inside,
        beyond,
    )
    for out, at in ((near, 96 - 96 * info[2]), (far, 96 * info[2])):
        rows = pl.ds(pl.multiple_of(at, 32), 32)
        for n in range(6):
            piece = shown[n][rows]
            out[n] = jnp.where(info[3] > 0, piece, 0.0) if n == 5 else piece


def step_kernel(info, main, inside, beyond, rows_in, rows_out, *refs):
    rec, groups, refs = refs[0], (refs[1:9], refs[9:17]), refs[17:]
    out, region, e, p, r, total = refs
    qx, qy = info[1], info[2]
    for z in range(4):
        region[z, 32:160] = main[z]
    region[4, 32:160] = inside[...]
    region[5, 32:160] = jnp.where(info[3] > 0, beyond[...], 0.0)
    for n in range(6):
        region[n, pl.ds(pl.multiple_of(160 * (1 - qy), 32), 32)] = rows_in[n]
        region[n, pl.ds(pl.multiple_of(160 * qy, 32), 32)] = jnp.where(
            info[4] > 0, rows_out[n], 0.0
        )
    spread(region, e, qx)
    for s in range(2):
        clear(p.at[s], 192)
        clear(r.at[s], 160)
    total[...] = jnp.zeros_like(total)
    masks = row_masks(info)
    far160, far128 = far_mask(160, qx), far_mask(128, qx)
    for pair in range(2):
        mats = groups[pair]
        for s in range(2):
            slot = 2 * pair + s

            def put(where, value):
                take_ratio(slot, rec, r.at[s], masks, where, value)

            near, edge = forward(s, qy, e, mats, p.at[s], put)
            put(slice(512, 640), jnp.where(far160, edge, near))
            planes, near, edge = adjoint(s, mats, r.at[s], total)
            finish(s, mats, planes, jnp.where(far128, edge, near), total)
    update(False, main, slice(0, 128), total, out, None, qx)


def make_matrices(one, two, after=None):
    return call(
        matrices_kernel,
        (
            shape(2, 2, 256, 256, dtype=BF16),
            shape(2, 2, 256, 256, dtype=BF16),
            shape(2, 256, 128, dtype=BF16),
            shape(2, 256, 128, dtype=BF16),
            shape(2, 2, 320, 256, dtype=BF16),
            shape(2, 2, 256, 256, dtype=BF16),
            shape(2, 2, 8, 128),
            shape(2, 2, 16, 128),
        ),
        [],
        one,
        two,
        flops=1_000_000_000,
        kept_out=range(8),
        after=after,
    )


def per_device(initial, recorded, tap_table, variants):
    count_tiles = lax.axis_size("tile")
    grid_rows = count_tiles // GX

    def route(x, pairs):
        return lax.ppermute(x, ("tile", "view"), pairs)

    def over_view(x, flip):
        return lax.ppermute(x, "view", [(i, i ^ flip) for i in range(4)])

    x_pairs, y_pairs = [], []
    for t in range(count_tiles):
        for v in range(4):
            me, right, below = 4 * t + v, 4 * (t + 1) + v - 2, 4 * (t + GX) + v - 1
            if v // 2 and t % GX < GX - 1:
                x_pairs += [(me, right), (right, me)]
            if v % 2 and t + GX < count_tiles:
                y_pairs += [(me, below), (below, me)]
            if t % GX == (GX - 1 if v // 2 else 0):
                x_pairs.append((me, 4 * t + (v ^ 1)))
            if t // GX == (grid_rows - 1 if v % 2 else 0):
                y_pairs.append((me, 4 * t + (v ^ 2)))

    sent = call(
        functools.partial(send_kernel, grid_rows),
        (shape(664, 128),) * 4,
        [
            VMEM((3, 8, 31), F32),
            SMEM((1, count_tiles), jnp.int32),
            VMEM((4, 256, 256), F32),
            pltpu.SemaphoreType.DMA((6,)),
        ],
        recorded[0, 0],
        tap_table[0].transpose(1, 0, 2),
        variants,
        in_place=(0, 1, 2),
    )
    got = [sent[0]] + [over_view(sent[s], s) for s in (1, 2, 3)]
    main, inside, edge = call(
        start_kernel,
        (shape(4, 160, 128), shape(160, 128), shape(160, 128)),
        [],
        initial[0],
    )
    start_cols = route(edge, x_pairs)
    mats = [make_matrices(*got[:2])]
    start_cols, mats[0] = lax.optimization_barrier((start_cols, mats[0]))
    start_rows = route(
        call(start_rows_kernel, shape(192, 128), [], main, inside, start_cols), y_pairs
    )
    e = call(
        region_kernel,
        shape(2, 4, 192, 256, dtype=BF16),
        [VMEM((6, 192, 128), F32)],
        main,
        inside,
        start_cols,
        start_rows,
    )

    def blur(parts, after, *groups):
        return call(
            functools.partial(forward_kernel, parts),
            shape(len(parts), 160, 640),
            [VMEM((len(parts), 2, 256, 640), BF16)],
            e,
            *groups,
            flops=1_000_000_000 * len(parts),
            kept_in=range(1, 1 + len(groups)),
            after=after,
        )

    packed_cols = call(pack_cols_kernel, shape(288, 128), [], *got, after=e)
    cols = route(packed_cols, x_pairs)
    mats.append(make_matrices(*got[2:], after=packed_cols))
    blurs = [blur(((0, 0),), packed_cols, *mats[0])]
    packed_rows = call(pack_rows_kernel, shape(320, 128), [], *got, cols, after=blurs[0])
    rows = route(packed_rows, y_pairs)
    blurs.append(blur(((0, 1), (1, 0), (1, 1)), packed_rows, *mats[0], *mats[1]))
    quad = shape(4, 128, 128)
    flat = [*mats[0], *mats[1]]
    estimate, near_edge, far_edge, rec = call(
        adjoint_kernel,
        (quad, shape(128, 128), shape(128, 128), shape(4, 160, 640)),
        [
            VMEM((2, 2, 256, 640), BF16),
            VMEM((4, 128, 128), F32),
        ],
        main,
        cols,
        rows,
        *got,
        *blurs,
        *flat,
        flops=4_000_000_000,
        kept_in=range(9, 25),
        kept_out=(3,),
    )
    for step in range(1, ITERS):
        inside = over_view(near_edge, 2)
        beyond = route(far_edge, x_pairs)
        near, far = call(
            mid_rows_kernel, (shape(6, 32, 128),) * 2, [], estimate, inside, beyond
        )
        rows_in = over_view(near, 1)
        rows_out = route(far, y_pairs)
        estimate = call(
            step_kernel,
            quad,
            [
                VMEM((6, 192, 128), F32),
                VMEM((2, 4, 192, 256), BF16),
                VMEM((2, 2, 256, 640), BF16),
                VMEM((2, 2, 256, 640), BF16),
                VMEM((4, 128, 128), F32),
            ],
                estimate,
            inside,
            beyond,
            rows_in,
            rows_out,
            rec,
            *flat,
            flops=8_000_000_000,
            kept_in=range(5, 22),
        )
    view = lax.axis_index("view")
    qx, qy = view // 2, view % 2
    across, down = over_view(estimate, 2), over_view(estimate, 1)
    corner = over_view(across, 1)
    top = jnp.where(qx == 0, *(jnp.concatenate(p, 2) for p in ((estimate, across), (across, estimate))))
    low = jnp.concatenate([down, down], 2)
    result = jnp.where(qy == 0, *(jnp.concatenate(p, 1) for p in ((top, low), (low, top))))
    zero = jnp.zeros((), jnp.int32)
    place = (zero, 128 * (1 - qy), 128 * (1 - qx))
    return lax.dynamic_update_slice(result, corner, place)[None]


def solution(mesh):
    return jax.shard_map(
        per_device,
        mesh=mesh,
        in_specs=(
            P("tile", None, None, None),
            P("view", "tile", None, None, None),
            P("view", None, None, None),
            P("view", None),
        ),
        out_specs=P("tile", None, None, None),
        check_vma=False,
    )
```

```python
import functools

import jax
import jax.numpy as jnp
from jax import lax
from jax.experimental import pallas as pl
from jax.experimental.pallas import tpu as pltpu
from jax.sharding import PartitionSpec as P

GX = 8
ITERS = 2
HALF = 15
F32 = jnp.float32
BF16 = jnp.bfloat16
VMEM = pltpu.VMEM
HBM = pltpu.MemorySpace.HBM
SMEM = pltpu.SMEM


def position():
    tile, view = lax.axis_index("tile"), lax.axis_index("view")
    qx, qy = lax.shift_right_logical(view, 1), jnp.bitwise_and(view, 1)
    col, row = lax.rem(tile, GX), lax.div(tile, GX)
    last = lax.axis_size("tile") // GX - 1
    has_x = jnp.where(qx == 0, col, GX - 1 - col)
    has_y = jnp.where(qy == 0, row, last - row)
    return view, qx, qy, has_x, has_y


def call(body, outs, scratch, *args, flops=0, in_place=(), kept_in=(), kept_out=(), after=None, limit=24):
    specs = [
        pl.BlockSpec(memory_space=HBM if n in in_place else VMEM) for n in range(len(args))
    ]
    args = list(args)
    for n in in_place:
        args[n] = pltpu.with_memory_space_constraint(args[n], HBM)
    for n in kept_in:
        args[n] = pltpu.with_memory_space_constraint(args[n], VMEM)
    plain = body
    if after is not None:
        specs.append(pl.BlockSpec(memory_space=pl.ANY))
        args.append(after)

        def body(info, *refs):
            plain(info, *refs[: len(args) - 1], *refs[len(args) :])

    moved = sum(a.size * a.dtype.itemsize for a in args)
    leaves = [
        VMEM(a.shape, a.dtype) if n in kept_out else a for n, a in enumerate(jax.tree.leaves(outs))
    ]
    return pl.pallas_call(
        lambda *refs: body(position(), *refs),
        out_shape=jax.tree.unflatten(jax.tree.structure(outs), leaves),
        in_specs=specs,
        out_specs=jax.tree.map(lambda _: pl.BlockSpec(memory_space=VMEM), outs),
        scratch_shapes=scratch,
        compiler_params=pltpu.CompilerParams(vmem_limit_bytes=limit * 1024 * 1024),
        cost_estimate=pl.CostEstimate(flops=flops, bytes_accessed=moved, transcendentals=0),
    )(*args)


def shape(*dims, dtype=F32):
    return jax.ShapeDtypeStruct(dims, dtype)


def lanes(rows, width=128):
    return lax.broadcasted_iota(jnp.int32, (rows, width), 1)


def turn(x, amount):
    if isinstance(amount, int):
        amount = amount % x.shape[-1]
        if amount == 0:
            return x
    return pltpu.roll(x, amount, axis=x.ndim - 1)


def packed(pieces, first, width):
    rows = pieces[0].shape[0]
    lane = lanes(rows)
    out = jnp.zeros((rows, 128), F32)
    for n, piece in enumerate(pieces):
        inside = (lane >= n * width) & (lane < (n + 1) * width)
        out = jnp.where(inside, turn(piece, n * width - first), out)
    return out


def right_half(rows):
    return lax.rem(lanes(rows), 32) < 16


def shared(pieces, qx):
    rows = pieces[0].shape[0]
    lane = lanes(rows)
    out = jnp.zeros((rows, 128), F32)
    for z, piece in enumerate(pieces):
        mine = turn(piece, lax.rem(32 * z + 32 * qx, 128))
        out = jnp.where((lane >= 32 * z) & (lane < 32 * z + 32), mine, out)
    return jnp.where(right_half(rows) == (qx == 0), out, 0.0)


def split(x):
    high = x.astype(BF16)
    return high, (x - high.astype(F32)).astype(BF16)


def dot3(stacked, high, low):
    rows = stacked.shape[0] // 2
    both = jnp.dot(stacked, high, preferred_element_type=F32)
    rest = jnp.dot(stacked[:rows], low, preferred_element_type=F32)
    return both[:rows] + (both[rows:] + rest)


def send_kernel(grid_rows, info, rec, table, variants, *refs):
    sent, (raw, ids, whole, sems) = refs[:4], refs[4:]
    loads = [pltpu.make_async_copy(rec.at[z], whole.at[z], sems.at[z]) for z in range(4)]
    small = [
        pltpu.make_async_copy(table, raw, sems.at[4]),
        pltpu.make_async_copy(variants, ids, sems.at[5]),
    ]
    for load in (*small, *loads):
        load.start()
    tile, view = lax.axis_index("tile"), lax.axis_index("view")
    row, col = lax.div(tile, GX), lax.rem(tile, GX)
    places = []
    for s in range(4):
        q = jnp.bitwise_xor(view, s)
        qx, qy = lax.shift_right_logical(q, 1), jnp.bitwise_and(q, 1)
        rows = pl.ds(pl.multiple_of(128 * qy, 128), 128)
        here = pl.ds(pl.multiple_of(128 * qx, 128), 128)
        there = pl.ds(pl.multiple_of(128 - 128 * qx, 128), 128)
        places.append((qx, qy, rows, here, there))
    for load in small:
        load.wait()
    raw[...] = raw[...] / jnp.sum(raw[...], axis=-1, keepdims=True)
    for s, (qx, qy, _, _, _) in enumerate(places):
        sent[s][576:592] = jnp.zeros((16, 128), F32)
        for n in range(4):
            x = jnp.clip(col + (2 * qx - 1) * (n % 2), 0, GX - 1)
            y = jnp.clip(row + (2 * qy - 1) * (n // 2), 0, grid_rows - 1)
            which = ids[0, y * GX + x]
            for axis in range(3):
                at = 576 + 3 * n + axis
                sent[s][at : at + 1, 0:31] = raw[axis, pl.ds(which, 1)]
    for z in range(4):
        loads[z].wait()
        for s, (_, _, rows, here, _) in enumerate(places):
            sent[s][128 * z : 128 * z + 128] = whole[z, rows, here]
    for s, (qx, _, rows, _, there) in enumerate(places):
        side = shared([whole[z, rows, there] for z in range(4)], qx)
        sent[s][512:576] = side[:64] + turn(side[64:], 16 + 96 * qx)


def own_side(block, qx):
    side = block[512:576]
    mine = right_half(64) == (qx == 0)
    low = jnp.where(mine, turn(side, 112 - 96 * qx), 0.0)
    return jnp.concatenate([jnp.where(mine, side, 0.0), low], 0)


def start_kernel(info, first, main, inside, edge):
    view = info[0]
    for q in range(4):
        qx, qy = q // 2, q % 2

        @pl.when(view == q)
        def _():
            span = slice(96 * qy, 96 * qy + 160)
            own = [first[z, span, 128 * qx : 128 * qx + 128] for z in range(4)]
            for z in range(4):
                main[z] = own[z]
            beside = [first[z, span, 128 - 128 * qx : 256 - 128 * qx] for z in range(4)]
            inside[...] = packed(beside, 96 * qx, 32)
            edge[...] = packed(own, 96 * qx, 32)


def pack_cols_kernel(info, *refs):
    got, out = refs[:4], refs[4]
    qx = info[1]
    for h in range(2):
        cols = []
        for s in (2 * h, 2 * h + 1):
            block = got[s ^ 2]
            cols.append(shared([block[128 * z : 128 * z + 128] for z in range(4)], qx))
        other = turn(cols[1], 16 + 96 * qx)
        out[h * 128 : h * 128 + 128] = cols[0] + other


def both_sides(inner, cols, odd, qx):
    rows = inner.shape[0]
    if odd:
        cols = turn(cols, 16 + 96 * qx)
    return jnp.where(right_half(rows) == (qx == 0), inner, cols)


def pack_rows_kernel(far, info, *refs):
    got, cols, out = refs[:4], refs[4], refs[5]
    qx, qy = info[1], info[2]
    sides = [own_side(got[s], qx) for s in range(4)]
    start = 112 * qy if far else 112 - 112 * qy
    at = pl.multiple_of(start, 16)
    for s in range(4):
        o = s ^ 1
        for z in range(4):
            n = 4 * s + z
            out[n * 16 : n * 16 + 16] = got[o][pl.ds(128 * z + at, 16)]
        inner = jnp.where(start == 0, sides[o][:16], sides[o][112:])
        outer = cols[pl.ds((o // 2) * 128 + at, 16)]
        out[256 + 16 * s : 272 + 16 * s] = both_sides(inner, outer, o % 2, qx)


def start_rows_kernel(info, main, inside, cols, out):
    at = pl.multiple_of(128 * info[2], 32)
    for z in range(4):
        out[32 * z : 32 * z + 32] = main[z, pl.ds(at, 32)]
    out[128:160] = inside[pl.ds(at, 32)]
    out[160:192] = jnp.where(info[3] > 0, cols[pl.ds(at, 32)], 0.0)


def toeplitz(base, shift):
    return pltpu.roll(base, shift % 256, axis=1, stride=1, stride_axis=0)


def matrices_kernel(info, one, two, xh, xl, ah, al, y, t, zm, zs):
    qx, qy = info[1], info[2]
    for s, table in enumerate((one, two)):
        fwd = table[576:592]
        flip = lax.broadcasted_iota(jnp.int32, (128, 128), 0) + lanes(128) == 30
        rev = jnp.dot(fwd, flip.astype(F32), precision=lax.Precision.HIGHEST)
        zero = jnp.zeros((16, 128), F32)
        fwd = jnp.concatenate([fwd, zero], 1)
        rev = jnp.concatenate([rev, zero], 1)

        def wide(which, tile, axis, rows):
            return jnp.broadcast_to(which[3 * tile + axis : 3 * tile + axis + 1], (rows, 256))

        lane = lanes(256)
        right, left = lane < 16, (lane >= 16) & (lane < 32)
        for g in range(2):
            near_t = toeplitz(wide(rev, 2 * g, 0, 256), -HALF)
            far_t = toeplitz(wide(rev, 2 * g + 1, 0, 256), -HALF)
            rhs = jnp.where(qx == 1, far_t[:, 128:], near_t[:, 128:])
            lhs = jnp.where(qx == 0, far_t[:, 128:], near_t[:, 128:])
            side = jnp.where(right, rhs, jnp.where(left, turn(lhs, 32), 0.0))
            xh[s, g], xl[s, g] = split(jnp.concatenate([near_t[:, :128], side], 1))
        row = lax.broadcasted_iota(jnp.int32, (256, 256), 0)
        far_row = (row >= 128) & ((row < 192) == (qx == 1))
        base = jnp.where(far_row, wide(fwd, 1, 0, 256), wide(fwd, 0, 0, 256))
        adj = toeplitz(base, -HALF)[:, :128]
        adj = jnp.concatenate(
            [adj[:144], adj[240:], jnp.zeros((96, 128), F32)], 0
        )
        ah[s], al[s] = split(adj)
        for g in range(2):
            row = lax.broadcasted_iota(jnp.int32, (160, 256), 0)
            other = jnp.where(qy == 0, row, 159 - row) < 16
            base = jnp.where(other, wide(fwd, 2 + g, 1, 160), wide(fwd, g, 1, 160))
            y[s, g, :160], y[s, g, 160:] = split(toeplitz(base, 1))
            wider = lanes(128, 256)
            other = jnp.where(qy == 0, wider, 159 - wider) < 16
            near_t = toeplitz(wide(rev, g, 1, 128), 1)
            far_t = toeplitz(wide(rev, 2 + g, 1, 128), 1)
            t[s, g, :128], t[s, g, 128:] = split(jnp.where(other, far_t, near_t))
        lane = lanes(1)
        plane = lax.div(lane, 32)
        far = right_half(1) == (qx == 1)
        for g in range(2):
            near_w = [
                jnp.broadcast_to(fwd[6 * g + 2 : 6 * g + 3, c : c + 1], (1, 128))
                for c in range(12, 19)
            ]
            far_w = [
                jnp.broadcast_to(fwd[6 * g + 5 : 6 * g + 6, c : c + 1], (1, 128))
                for c in range(12, 19)
            ]
            for d in range(7):
                zm[s, g, d : d + 1] = near_w[d]
                inside = (plane + (d - 3) >= 0) & (plane + (d - 3) < 4)
                for adjoint in range(2):
                    c = 6 - d if adjoint else d
                    value = jnp.where(far, far_w[c], near_w[c])
                    at = 8 * adjoint + d
                    zs[s, g, at : at + 1] = jnp.where(inside, value, 0.0)


def sided(left, right, width, n, rows):
    lane = lanes(rows)
    out = jnp.where(lane < width, turn(right, -n * width), 0.0)
    return jnp.where(lane >= 128 - width, turn(left, 128 - width - n * width), out)


def spread(region, e, qx):
    left = jnp.where(qx == 0, region[5], region[4])
    right = jnp.where(qx == 0, region[4], region[5])
    for z in range(4):
        e[0, z, :, :128], e[1, z, :, :128] = split(region[z])
        e[0, z, :, 128:], e[1, z, :, 128:] = split(sided(left, right, 32, z, 192))


def region_kernel(info, main, inside, cols, rows_in, e, region):
    own = pl.multiple_of(32 * (1 - info[2]), 32)
    other = pl.multiple_of(160 * info[2], 32)
    for z in range(4):
        region[z, pl.ds(own, 160)] = main[z]
    for n in range(6):
        region[n, pl.ds(other, 32)] = jnp.where(
            info[4] > 0, rows_in[32 * n : 32 * n + 32], 0.0
        )
    region[4, pl.ds(own, 160)] = inside[...]
    region[5, pl.ds(own, 160)] = jnp.where(info[3] > 0, cols[...], 0.0)
    spread(region, e, info[1])


def mix_planes(planes, side, main_w, side_w, adjoint):
    out = []
    for z in range(4):
        order = [3 + z - k if adjoint else 3 + k - z for k in range(4)]
        out.append(sum(main_w[order[k]] * planes[k] for k in range(4)))
    out.append(sum(side_w[d] * turn(side, -32 * (d - 3)) for d in range(7)))
    return out


def forward(s, qy, e, mats, p, put):
    xh, xl, _, _, y, _, zm, zs = mats
    own = pl.multiple_of(32 * (1 - qy), 32)
    other = pl.multiple_of(160 * qy, 32)
    for g, at, count in ((0, own, 160), (1, other, 32)):
        planes, side = [], None
        for z in range(4):
            here = jnp.concatenate([e[0, z, pl.ds(at, count)], e[1, z, pl.ds(at, count)]], 0)
            value = dot3(here, xh[s, g], xl[s, g])
            planes.append(value[:, :128])
            moved = turn(value[:, 128:], 32 * z)
            side = moved if side is None else side + moved
        main_w = [zm[s, g, d : d + 1] for d in range(7)]
        side_w = [zs[s, g, d : d + 1] for d in range(7)]
        for z, value in enumerate(mix_planes(planes, side, main_w, side_w, False)):
            here = slice(128 * z, 128 * z + 128)
            p[0, pl.ds(at, count), here], p[1, pl.ds(at, count), here] = split(value)
    for a in (0, 256):
        put(slice(a, a + 256), dot3(y[s, 0], p[0, :, a : a + 256], p[1, :, a : a + 256]))
    high, low = p[0, :, 512:], p[1, :, 512:]
    near, edge = dot3(y[s, 0], high, low), dot3(y[s, 1], high, low)
    return near, edge


def adjoint(s, mats, r, total):
    _, _, ah, al, _, t, zm, zs = mats
    planes = []
    for a in (0, 256):
        pair = dot3(t[s, 0], r[0, :, a : a + 256], r[1, :, a : a + 256])
        planes += [pair[:, :128], pair[:, 128:]]
    high, low = r[0, :, 512:], r[1, :, 512:]
    return planes, dot3(t[s, 0], high, low), dot3(t[s, 1], high, low)


def finish(s, mats, planes, side, total):
    _, _, ah, al, _, _, zm, zs = mats
    main_w = [zm[s, 0, d : d + 1] for d in range(7)]
    side_w = [zs[s, 0, 8 + d : 9 + d] for d in range(7)]
    *planes, side = mix_planes(planes, side, main_w, side_w, True)
    for z in range(4):
        both = jnp.concatenate([planes[z], turn(side, -32 * z)], 1)
        correction = dot3(jnp.concatenate(split(both), 0), ah[s], al[s])
        total[z] += jnp.log(correction)


def far_mask(rows, qx):
    return right_half(rows) == (qx == 1)


def clear(ref, first):
    ref[:, first:] = jnp.zeros((2, 256 - first, 640), BF16)


def forward_kernel(parts, info, e, *refs):
    groups, (out, p) = (refs[:8], refs[8:-2]), refs[-2:]
    far = far_mask(160, info[1])
    for n, (group, s) in enumerate(parts):
        clear(p.at[n], 192)

        def put(where, value):
            out[n, :, where] = value

        near, edge = forward(s, info[2], e, groups[group], p.at[n], put)
        out[n, :, 512:] = jnp.where(far, edge, near)


def row_masks(info):
    row = lax.broadcasted_iota(jnp.int32, (160, 128), 0)
    past = jnp.where(info[2] == 0, row, 159 - row) < 16
    inside = (info[4] > 0) | ~past
    side = inside & ((info[3] > 0) | ~far_mask(160, info[1]))
    return inside, side


def take_ratio(s, rec, r, masks, where, blurred):
    wide = jnp.concatenate([masks[0], masks[0]], 1) if blurred.shape[1] == 256 else masks[1]
    ratio = jnp.where(wide, rec[s, :, where] / blurred, 0.0)
    r[0, :160, where], r[1, :160, where] = split(ratio)


def update(first, main, at, total, out, edges, qx):
    new = []
    for z in range(4):
        new.append(main[z, at] * jnp.exp(total[z] / 4))
        out[z] = new[z]
    if first:
        low, high = packed(new, 0, 32), packed(new, 96, 32)
        edges[0][...] = jnp.where(qx == 0, high, low)
        edges[1][...] = jnp.where(qx == 0, low, high)


def adjoint_kernel(info, main, cols, rows_near, rows_far, *refs):
    got, blurs, refs = refs[:4], refs[4:6], refs[6:]
    groups, refs = (refs[:8], refs[8:16]), refs[16:]
    out, near_edge, far_edge, rec, r, total = refs
    qx, qy = info[1], info[2]
    for s in range(4):
        for z in range(4):
            rec[s, 16:144, 128 * z : 128 * z + 128] = got[s][128 * z : 128 * z + 128]
        outer = cols[(s // 2) * 128 : (s // 2) * 128 + 128]
        rec[s, 16:144, 512:] = both_sides(own_side(got[s], qx), outer, s % 2, qx)
        for rows, start in ((rows_near, 144 * (1 - qy)), (rows_far, 144 * qy)):
            at = pl.ds(pl.multiple_of(start, 16), 16)
            for z in range(4):
                n = 4 * s + z
                rec[s, at, 128 * z : 128 * z + 128] = rows[n * 16 : n * 16 + 16]
            rec[s, at, 512:] = rows[256 + 16 * s : 272 + 16 * s]
    for s in range(4):
        clear(r.at[s], 160)
    total[...] = jnp.zeros_like(total)
    masks = row_masks(info)
    far = far_mask(128, qx)
    for pair in range(2):
        mats = groups[pair]

        for s in range(2):
            for a, b in ((0, 256), (256, 512), (512, 640)):
                slot = 2 * pair + s
                blurred = blurs[1][slot - 1, :, a:b] if slot else blurs[0][0, :, a:b]
                take_ratio(slot, rec, r.at[slot], masks, slice(a, b), blurred)
            planes, near, edge = adjoint(s, mats, r.at[slot], total)
            finish(s, mats, planes, jnp.where(far, edge, near), total)
    at = pl.ds(pl.multiple_of(32 * qy, 32), 128)
    update(True, main, at, total, out, (near_edge, far_edge), qx)


def mid_rows_kernel(far, info, main, inside, beyond, out):
    rows = pl.ds(pl.multiple_of(96 * info[2] if far else 96 - 96 * info[2], 32), 32)
    for z in range(4):
        out[z] = main[z, rows]
    out[4] = inside[rows]
    out[5] = jnp.where(info[3] > 0, beyond[rows], 0.0)
    if far:
        out[6:] = jnp.zeros((1, 32, 128), F32)


def step_kernel(info, main, inside, beyond, rows_in, rows_out, *refs):
    rec, groups, refs = refs[0], (refs[1:9], refs[9:17]), refs[17:]
    out, region, e, p, r, total = refs
    qx, qy = info[1], info[2]
    for z in range(4):
        region[z, 32:160] = main[z]
    region[4, 32:160] = inside[...]
    region[5, 32:160] = jnp.where(info[3] > 0, beyond[...], 0.0)
    for n in range(6):
        region[n, pl.ds(pl.multiple_of(160 * (1 - qy), 32), 32)] = rows_in[n]
        region[n, pl.ds(pl.multiple_of(160 * qy, 32), 32)] = jnp.where(
            info[4] > 0, rows_out[n], 0.0
        )
    spread(region, e, qx)
    for s in range(4):
        clear(p.at[s], 192)
        clear(r.at[s], 160)
    total[...] = jnp.zeros_like(total)
    masks = row_masks(info)
    far160, far128 = far_mask(160, qx), far_mask(128, qx)
    for pair in range(2):
        mats = groups[pair]
        for s in range(2):
            slot = 2 * pair + s

            def put(where, value):
                take_ratio(slot, rec, r.at[slot], masks, where, value)

            near, edge = forward(s, qy, e, mats, p.at[slot], put)
            put(slice(512, 640), jnp.where(far160, edge, near))
            planes, near, edge = adjoint(s, mats, r.at[slot], total)
            finish(s, mats, planes, jnp.where(far128, edge, near), total)
    update(False, main, slice(0, 128), total, out, None, qx)


def make_matrices(one, two, after=None):
    return call(
        matrices_kernel,
        (
            shape(2, 2, 256, 256, dtype=BF16),
            shape(2, 2, 256, 256, dtype=BF16),
            shape(2, 256, 128, dtype=BF16),
            shape(2, 256, 128, dtype=BF16),
            shape(2, 2, 320, 256, dtype=BF16),
            shape(2, 2, 256, 256, dtype=BF16),
            shape(2, 2, 8, 128),
            shape(2, 2, 16, 128),
        ),
        [],
        one,
        two,
        flops=1_000_000_000,
        kept_out=range(8),
        after=after,
    )


def per_device(initial, recorded, tap_table, variants):
    count_tiles = lax.axis_size("tile")
    grid_rows = count_tiles // GX

    def route(x, pairs):
        return lax.ppermute(x, ("tile", "view"), pairs)

    def over_view(x, flip):
        return lax.ppermute(x, "view", [(i, i ^ flip) for i in range(4)])

    x_pairs, y_pairs = [], []
    for t in range(count_tiles):
        for v in range(4):
            me, right, below = 4 * t + v, 4 * (t + 1) + v - 2, 4 * (t + GX) + v - 1
            if v // 2 and t % GX < GX - 1:
                x_pairs += [(me, right), (right, me)]
            if v % 2 and t + GX < count_tiles:
                y_pairs += [(me, below), (below, me)]
            if t % GX == (GX - 1 if v // 2 else 0):
                x_pairs.append((me, 4 * t + (v ^ 1)))
            if t // GX == (grid_rows - 1 if v % 2 else 0):
                y_pairs.append((me, 4 * t + (v ^ 2)))

    sent = call(
        functools.partial(send_kernel, grid_rows),
        (shape(592, 128),) * 4,
        [
            VMEM((3, 8, 31), F32),
            SMEM((1, count_tiles), jnp.int32),
            VMEM((4, 256, 256), F32),
            pltpu.SemaphoreType.DMA((6,)),
        ],
        recorded[0, 0],
        tap_table[0].transpose(1, 0, 2),
        variants,
        in_place=(0, 1, 2),
    )
    got = [sent[0]] + [over_view(sent[s], s) for s in (1, 2, 3)]
    main, inside, edge = call(
        start_kernel,
        (shape(4, 160, 128), shape(160, 128), shape(160, 128)),
        [],
        initial[0],
    )
    start_cols = route(edge, x_pairs)
    mats = [make_matrices(*got[:2])]
    start_cols, mats[0] = lax.optimization_barrier((start_cols, mats[0]))
    start_rows = route(
        call(start_rows_kernel, shape(192, 128), [], main, inside, start_cols), y_pairs
    )
    e = call(
        region_kernel,
        shape(2, 4, 192, 256, dtype=BF16),
        [VMEM((6, 192, 128), F32)],
        main,
        inside,
        start_cols,
        start_rows,
    )

    def blur(parts, after, *groups):
        return call(
            functools.partial(forward_kernel, parts),
            shape(len(parts), 160, 640),
            [VMEM((len(parts), 2, 256, 640), BF16)],
            e,
            *groups,
            flops=1_000_000_000 * len(parts),
            kept_in=range(1, 1 + len(groups)),
            after=after,
        )

    packed_cols = call(pack_cols_kernel, shape(256, 128), [], *got, after=e)
    cols = route(packed_cols, x_pairs)
    mats.append(make_matrices(*got[2:], after=packed_cols))
    blurs = [blur(((0, 0),), packed_cols, *mats[0])]
    pack_rows = [functools.partial(pack_rows_kernel, far) for far in (True, False)]
    packed_rows = call(pack_rows[0], shape(320, 128), [], *got, cols, after=blurs[0])
    rows = route(packed_rows, y_pairs)
    inner_rows = call(pack_rows[1], shape(320, 128), [], *got, cols, after=packed_rows)
    rows_near = over_view(inner_rows, 1)
    blurs.append(blur(((0, 1), (1, 0), (1, 1)), inner_rows, *mats[0], *mats[1]))
    quad = shape(4, 128, 128)
    flat = [*mats[0], *mats[1]]
    estimate, near_edge, far_edge, rec = call(
        adjoint_kernel,
        (quad, shape(128, 128), shape(128, 128), shape(4, 160, 640)),
        [
            VMEM((4, 2, 256, 640), BF16),
            VMEM((4, 128, 128), F32),
        ],
        main,
        cols,
        rows_near,
        rows,
        *got,
        *blurs,
        *flat,
        flops=4_000_000_000,
        kept_in=range(10, 26),
        kept_out=(3,),
    )
    for step in range(1, ITERS):
        inside = over_view(near_edge, 2)
        beyond = route(far_edge, x_pairs)
        mid_rows = [functools.partial(mid_rows_kernel, far) for far in (True, False)]
        far_rows = call(mid_rows[0], shape(7, 32, 128), [], estimate, inside, beyond)
        rows_out = route(far_rows, y_pairs)
        near_rows = call(
            mid_rows[1],
            shape(6, 32, 128),
            [],
            estimate,
            inside,
            beyond,
            after=far_rows,
            flops=2_000_000_000,
        )
        rows_in = over_view(near_rows, 1)
        estimate = call(
            step_kernel,
            quad,
            [
                VMEM((6, 192, 128), F32),
                VMEM((2, 4, 192, 256), BF16),
                VMEM((4, 2, 256, 640), BF16),
                VMEM((4, 2, 256, 640), BF16),
                VMEM((4, 128, 128), F32),
            ],
                estimate,
            inside,
            beyond,
            rows_in,
            rows_out,
            rec,
            *flat,
            flops=8_000_000_000,
            kept_in=range(5, 22),
        )
    view = lax.axis_index("view")
    qx, qy = view // 2, view % 2
    across, down = over_view(estimate, 2), over_view(estimate, 1)
    corner = over_view(across, 1)
    top = jnp.where(qx == 0, *(jnp.concatenate(p, 2) for p in ((estimate, across), (across, estimate))))
    low = jnp.concatenate([down, down], 2)
    result = jnp.where(qy == 0, *(jnp.concatenate(p, 1) for p in ((top, low), (low, top))))
    zero = jnp.zeros((), jnp.int32)
    place = (zero, 128 * (1 - qy), 128 * (1 - qx))
    return lax.dynamic_update_slice(result, corner, place)[None]


def solution(mesh):
    return jax.shard_map(
        per_device,
        mesh=mesh,
        in_specs=(
            P("tile", None, None, None),
            P("view", "tile", None, None, None),
            P("view", None, None, None),
            P("view", None),
        ),
        out_specs=P("tile", None, None, None),
        check_vma=False,
    )
```
